32 devices in a mesh: chain: 2 (over y), cell: 4 (over z), col: 4 (over x, core).
Axes of the slice: x: 2, y: 2, z: 4, core: 2. Of those that a mesh axis runs over, the one named last changes fastest.
Arguments:
- grad: float32 [16384, 64], P(('chain', 'cell', 'col')), parts along dimension 0, may hold values from -6 to 6
- near_tiles: bfloat16 [4, 2, 2048, 2048], P('cell', None, 'col'), may hold values from -0.09375 to 0.09375
- tile_count: int32 [4], replicated, may hold values from 1 to 2
- near_offset: int32 [4], replicated, may hold values from -2 to 2, as said below
- far_src: int32 [4, 8], replicated, may hold values from 0 to 3
- far_count: int32 [4], replicated, may hold values from 1 to 8
- far_cores: float32 [4, 8, 64, 64], P('cell'), may hold values from -0.25 to 0.25
- basis_out: bfloat16 [8192, 64], P(('cell', 'col')), may hold values from -0.75 to 0.75
- basis_in: bfloat16 [8192, 64], P(('cell', 'col')), may hold values from -0.125 to 0.125
Outputs:
- step_block: float32 [16384, 64], P(('chain', 'cell', 'col')), parts along dimension 0
The draws below stay inside these ranges and needn't reach their ends.
There are 2 independent parts, one for each index of `chain`. The reference program is written for one: setup_inputs(seed, part) draws one part's arguments, and reference() takes and returns one part's arrays. A program takes and returns all parts, laid end to end along the dimension named above; an argument that names none is the same for every part. Nothing has to cross between parts.
Inputs may be any that keep to these rules, and one draw needn't show every extreme that they name: c + near_offset[c] is a cluster of the chain, and near_offset[c] is never 0.
All inputs are finite; a program needn't handle non-finite values.
Results may differ from the reference program's by a relative error of at most 0.0035.
Values may be sent and summed in bfloat16 or wider, within the bound.
No kernel may reach another device: no remote copies, remote signals or barrier semaphores. Data moves between devices by JAX's collectives and lax.ppermute only.
A program may use at most 64 MiB of HBM per device.

```python
import jax
import jax.numpy as jnp
from jax import lax

CLUS = 2048
COLS = 64
RANK = 64
NEAR = 2
FAR = 8
NCLUS = 4
CELLS = 8192


def draw_near_offset(key, part):
    pick = jax.random.randint(key, (NCLUS,), 0, 4)
    table = jnp.array([-2, -1, 1, 2], jnp.int32)
    offset = table[pick]
    index = jnp.arange(NCLUS, dtype=jnp.int32)
    target = index + offset
    outside = (target < 0) | (target >= NCLUS)
    return jnp.where(outside, -offset, offset).astype(jnp.int32)


def with_ends(values, key, low, high):
    longest = values.shape.index(max(values.shape))
    spots = []
    for shift in (0, 1):
        where = [jax.random.randint(jax.random.fold_in(key, axis), (), 0, length) for axis, length in enumerate(values.shape)]
        where[longest] = (where[longest] + shift) % values.shape[longest]
        spots.append(tuple(where))
    return values.at[spots[0]].set(low).at[spots[1]].set(high)


def block_levels(rng, dims, shards, smallest, high):
    def one(axis_at, parts):
        steps = jax.random.uniform(jax.random.fold_in(jax.random.fold_in(rng, 6), axis_at), (parts,), jnp.float32, smallest / len(shards), high / len(shards))
        return jnp.repeat(jnp.exp(steps), dims[axis_at] // parts).reshape((-1,) + (1,) * (len(dims) - axis_at - 1))

    gain = one(*shards[0])
    for cut in shards[1:]:
        gain = gain * one(*cut)
    return gain


def gaussian(own_key, shape, scale, most, shards=(), kind=jnp.bfloat16):
    gain = block_levels(own_key, shape, shards, -0.22, 0.18) if shards else 1.0
    values = jax.random.normal(own_key, shape, jnp.float32) * scale * gain
    return jnp.minimum(jnp.maximum(values, -most), most).astype(kind)


def setup_inputs(seed: int = 0, part: int = 0) -> dict:
    key_of = jax.random.split(jax.random.key(seed), 10)
    part_keys = jax.random.split(jax.random.fold_in(key_of[9], part), 10)
    grad = gaussian(part_keys[0], (CELLS, COLS), 1.0, 6.0, ((0, 16),), jnp.float32)
    near_tiles = gaussian(key_of[1], (NCLUS, NEAR, CLUS, CLUS), (2 * CLUS) ** -0.5, 0.09375, ((0, 4), (2, 4)))
    tile_count = with_ends(jax.random.randint(key_of[2], (NCLUS,), 1, 3), jax.random.fold_in(key_of[2], 1), 1, 2).astype(jnp.int32)
    near_offset = draw_near_offset(jax.random.fold_in(key_of[9], 71), part)
    far_src = with_ends(jax.random.randint(key_of[4], (NCLUS, FAR), 0, NCLUS), jax.random.fold_in(key_of[4], 1), 0, NCLUS - 1).astype(jnp.int32)
    far_count = with_ends(jax.random.randint(key_of[5], (NCLUS,), 1, FAR + 1), jax.random.fold_in(key_of[5], 1), 1, FAR).astype(jnp.int32)
    far_cores = gaussian(key_of[6], (NCLUS, FAR, RANK, RANK), (RANK * FAR) ** -0.5, 0.25, ((0, 4),), jnp.float32)
    basis_out = gaussian(key_of[7], (CELLS, RANK), RANK ** -0.5, 0.75, ((0, 16),))
    basis_in = gaussian(key_of[8], (CELLS, RANK), CLUS ** -0.5, 0.125, ((0, 16),))
    return {"grad": grad, "near_tiles": near_tiles, "tile_count": tile_count, "near_offset": near_offset, "far_src": far_src, "far_count": far_count, "far_cores": far_cores, "basis_out": basis_out, "basis_in": basis_in}


def reference(grad, near_tiles, tile_count, near_offset, far_src, far_count, far_cores, basis_out, basis_in):
    rounded = grad.astype(jnp.bfloat16).reshape(NCLUS, CLUS, COLS)
    inbasis = basis_in.reshape(NCLUS, CLUS, RANK)
    outbasis = basis_out.reshape(NCLUS, CLUS, RANK)
    proj = jnp.einsum("cra,crw->caw", inbasis.astype(jnp.float32), rounded.astype(jnp.float32), precision=lax.Precision.HIGHEST)
    slots = jnp.arange(FAR, dtype=jnp.int32)

    def one_cluster(index):
        tiles = near_tiles[index]
        own = jnp.dot(tiles[0], rounded[index], preferred_element_type=jnp.float32)
        source = (index + near_offset[index]).astype(jnp.int32)
        other = jnp.dot(tiles[1], rounded[source], preferred_element_type=jnp.float32)
        near = own + jnp.where(tile_count[index] == 2, other, jnp.zeros_like(other))
        picked = proj[far_src[index]]
        cores = jnp.where((slots < far_count[index])[:, None, None], far_cores[index], jnp.zeros_like(far_cores[index]))
        coupled = jnp.einsum("kab,kbw->aw", cores, picked, precision=lax.Precision.HIGHEST)
        far = jnp.dot(outbasis[index], coupled.astype(jnp.bfloat16), preferred_element_type=jnp.float32)
        return near + far

    result = lax.map(one_cluster, jnp.arange(NCLUS, dtype=jnp.int32))
    return result.reshape(NCLUS * CLUS, COLS)
```

```python
import functools

import jax
import jax.numpy as jnp
from jax import lax
from jax.experimental import pallas as pl
from jax.experimental.pallas import tpu as pltpu
from jax.sharding import PartitionSpec as P

REACH = 2
F32 = jnp.float32
BF16 = jnp.bfloat16
VMEM = pl.BlockSpec(memory_space=pltpu.VMEM)
SMEM = pl.BlockSpec(memory_space=pltpu.SMEM)
ANY = pl.BlockSpec(memory_space=pl.ANY)
NT = (((1,), (1,)), ((), ()))


def call(kernel, out, inputs, specs, scratch=(), flops=0, moved=0, name=None):
    return pl.pallas_call(
        kernel,
        out_shape=out,
        in_specs=specs,
        out_specs=jax.tree.map(lambda _: VMEM, out),
        scratch_shapes=list(scratch),
        cost_estimate=pl.CostEstimate(flops=flops, bytes_accessed=moved, transcendentals=0),
        compiler_params=pltpu.CompilerParams(vmem_limit_bytes=16 << 20),
        name=name,
    )(*inputs)


def split(value):
    high = value.astype(BF16)
    low = (value - high.astype(F32)).astype(BF16)
    return high, low


def join(ref, at, width):
    high = ref[:, at : at + width].astype(F32)
    return high + ref[:, at + width : at + 2 * width].astype(F32)


def first_kernel(grad_ref, basis_ref, out_ref):
    rank, rows = basis_ref.shape
    rounded = grad_ref[...].astype(BF16)
    out_ref[:, :rows] = rounded
    partial = lax.dot_general(rounded, basis_ref[...], NT, preferred_element_type=F32)
    high, low = split(partial)
    out_ref[:, rows : rows + rank] = high
    out_ref[:, rows + rank :] = low


def table_kernel(count_ref, offset_ref, source_ref, far_ref, cores_ref, mix_ref, flag_ref):
    owner = lax.axis_index("cell")
    slots, rank, _ = cores_ref.shape
    cells = mix_ref.shape[1] // rank
    used = far_ref[owner]
    for step in range(cells):
        total = jnp.zeros((rank, rank), F32)
        for slot in range(slots):
            hit = jnp.logical_and(source_ref[owner, slot] == (owner ^ step), slot < used)
            total = total + jnp.where(hit, cores_ref[slot], 0.0)
        mix_ref[:, step * rank : (step + 1) * rank] = total
    beyond = owner ^ 2
    asked = beyond + offset_ref[beyond] == owner ^ 1
    beside = offset_ref[owner] + owner == owner ^ 1
    double = count_ref[owner] == 2
    for row, value in enumerate((asked, beside, double)):
        flag_ref[row] = jnp.full(flag_ref.shape[1:], value.astype(F32), F32)


def pick(flag_ref, row, yes, no):
    shape = yes.shape
    mask = jnp.broadcast_to(flag_ref[row][:1, :1], shape) > 0.5
    return jnp.where(mask, yes.astype(F32), no.astype(F32)).astype(BF16)


def second_kernel(flag_ref, mine_ref, near_ref, out_ref, *, rows):
    out_ref[:, :rows] = pick(flag_ref, 0, near_ref[:, :rows], mine_ref[:, :rows])
    tail = mine_ref.shape[1] - rows
    out_ref[:, rows : rows + tail] = mine_ref[:, rows:]
    out_ref[:, rows + tail :] = near_ref[:, rows:]


def third_kernel(flag_ref, mix_ref, mine_ref, near_ref, far_ref, out_ref, *, rows):
    rank = mix_ref.shape[0]
    beside = pick(flag_ref, 1, near_ref[:, :rows], far_ref[:, :rows])
    beside = pick(flag_ref, 2, beside, jnp.zeros_like(beside))
    out_ref[:, :rows] = mine_ref[:, :rows]
    out_ref[:, rows : 2 * rows] = beside
    table = jnp.concatenate(
        (
            join(mine_ref, rows, rank),
            join(near_ref, rows, rank),
            join(far_ref, rows, rank),
            join(far_ref, rows + 2 * rank, rank),
        ),
        axis=1,
    )
    core = lax.dot_general(
        table, mix_ref[...], NT, precision=lax.Precision.HIGHEST, preferred_element_type=F32
    )
    high, low = split(core)
    out_ref[:, 2 * rows : 2 * rows + rank] = high
    out_ref[:, 2 * rows + rank :] = low


def widen_kernel(mine_ref, other_ref, out_ref, *, rank):
    body = mine_ref.shape[1] - 2 * rank
    out_ref[:, :body] = mine_ref[:, :body]
    out_ref[:, body : 2 * body] = other_ref[:, :body]
    high, low = split(join(mine_ref, body, rank) + join(other_ref, body, rank))
    out_ref[:, 2 * body : 2 * body + rank] = high
    out_ref[:, 2 * body + rank :] = low


def last_kernel(mine_ref, other_ref, basis_ref, tiles_ref, out_ref, buffer, sems, *, order):
    place = lax.axis_index("col")
    rank, rows = basis_ref.shape
    body = mine_ref.shape[1] - 2 * rank
    copies = []
    for item, (part, spot) in enumerate(order):
        columns = pl.ds(pl.multiple_of((place ^ spot) * rows, rows), rows)
        copy = pltpu.make_async_copy(
            tiles_ref.at[part, :, columns], buffer.at[item], sems.at[item]
        )
        copy.start()
        copies.append(copy)
    core = join(mine_ref, body, rank) + join(other_ref, body, rank)
    total = jnp.dot(core.astype(BF16), basis_ref[...], preferred_element_type=F32)
    half = len(order) // 2
    for item, copy in enumerate(copies):
        copy.wait()
        source = mine_ref if item < half else other_ref
        at = (item % half) * rows
        total = total + lax.dot_general(
            source[:, at : at + rows], buffer[item], NT, preferred_element_type=F32
        )
    out_ref[...] = total


def swap(value, axis, step):
    size = lax.axis_size(axis)
    return lax.ppermute(value, axis, [(i, i ^ step) for i in range(size)])


def shifted(value, axis, by):
    size = lax.axis_size(axis)
    return lax.ppermute(value, axis, [(i, i + by) for i in range(size) if 0 <= i + by < size])


def over_small_chain(first, tables, cores, rows):
    width, length = first.shape
    rank = cores.shape[1]
    near = swap(first, "cell", 1)
    mix, flags = call(
        table_kernel,
        (
            jax.ShapeDtypeStruct((rank, 4 * rank), F32),
            jax.ShapeDtypeStruct((3, 8, 128), F32),
        ),
        (*tables, cores),
        [SMEM] * 4 + [VMEM],
        moved=cores.size * 4,
        name="tables",
    )
    second = call(
        functools.partial(second_kernel, rows=rows),
        jax.ShapeDtypeStruct((width, 2 * length - rows), BF16),
        (flags, first, near),
        [VMEM] * 3,
        moved=4 * first.size,
        name="second",
    )
    far = swap(second, "cell", 2)
    return call(
        functools.partial(third_kernel, rows=rows),
        jax.ShapeDtypeStruct((width, length + rows), BF16),
        (flags, mix, first, near, far),
        [VMEM] * 5,
        moved=8 * first.size,
        name="third",
    )


def over_long_chain(first, tables, cores, rows):
    owner = lax.axis_index("cell")
    rank = cores.shape[1]
    counts, offsets, sources, used = (table[owner] for table in tables)
    steps = [step for step in range(-REACH, REACH + 1) if step]
    moved = jnp.stack([shifted(first[:, :rows], "cell", -step) for step in steps])
    beside = lax.dynamic_index_in_dim(
        moved, offsets + REACH - (offsets > 0).astype(jnp.int32), 0, keepdims=False
    )
    beside = jnp.where(counts == 2, beside, jnp.zeros_like(beside))
    high, low = first[:, rows : rows + rank], first[:, rows + rank :]
    partial = high.astype(F32) + low.astype(F32)
    table = lax.all_gather(partial[None], "cell", axis=0, tiled=True)
    picked = jnp.take(table, sources, axis=0)
    slots = jnp.arange(cores.shape[0], dtype=jnp.int32)
    masked = jnp.where((slots < used)[:, None, None], cores, jnp.zeros_like(cores))
    core = jnp.einsum("kab,kwb->wa", masked, picked, precision=lax.Precision.HIGHEST)
    return jnp.concatenate((first[:, :rows], beside, *split(core)), axis=1)


def body(
    grad, near_tiles, tile_count, near_offset, far_src, far_count, far_cores, basis_out, basis_in
):
    rows, width = grad.shape
    rank = basis_in.shape[1]
    cells, parts = lax.axis_size("cell"), lax.axis_size("col")
    first = call(
        first_kernel,
        jax.ShapeDtypeStruct((width, rows + 2 * rank), BF16),
        (grad.T, basis_in.T),
        [VMEM] * 2,
        moved=8 * grad.size,
        name="first",
    )
    tables = (tile_count, near_offset, far_src, far_count)
    over_cells = over_small_chain if cells == 2 * REACH else over_long_chain
    held = over_cells(first, tables, far_cores[0], rows)
    order = [(0, 0), (1, 0)]
    step = parts // 2
    while step > 1:
        other = swap(held, "col", step)
        held = call(
            functools.partial(widen_kernel, rank=rank),
            jax.ShapeDtypeStruct((width, 2 * held.shape[1] - 2 * rank), BF16),
            (held, other),
            [VMEM] * 2,
            moved=8 * held.size,
            name="widen",
        )
        order += [(part, spot ^ step) for part, spot in order]
        step //= 2
    other = swap(held, "col", 1)
    order += [(part, spot ^ 1) for part, spot in order]
    out = call(
        functools.partial(last_kernel, order=order),
        jax.ShapeDtypeStruct((width, rows), F32),
        (held, other, basis_out.T, near_tiles[0]),
        [VMEM] * 3 + [ANY],
        scratch=(
            pltpu.VMEM((len(order), rows, rows), BF16),
            pltpu.SemaphoreType.DMA((len(order),)),
        ),
        flops=2 * near_tiles.size * width,
        moved=2 * near_tiles.size,
        name="last",
    )
    return out.T


def solution(mesh):
    placed = (
        P(("chain", "cell", "col"), None),
        P("cell", None, "col", None),
        P(),
        P(),
        P(),
        P(),
        P("cell", None, None, None),
        P(("cell", "col"), None),
        P(("cell", "col"), None),
    )
    return jax.shard_map(
        body,
        mesh=mesh,
        in_specs=placed,
        out_specs=P(("chain", "cell", "col"), None),
        check_vma=False,
    )
```

```python
import functools

import jax
import jax.numpy as jnp
from jax import lax
from jax.experimental import pallas as pl
from jax.experimental.pallas import tpu as pltpu
from jax.sharding import PartitionSpec as P

REACH = 2
F32 = jnp.float32
BF16 = jnp.bfloat16
VMEM = pl.BlockSpec(memory_space=pltpu.VMEM)
HBM = pl.BlockSpec(memory_space=pltpu.HBM)
NT = (((1,), (1,)), ((), ()))


def call(kernel, out, inputs, specs, scratch=(), flops=0, moved=0, name=None):
    inputs = [
        pltpu.with_memory_space_constraint(value, pltpu.HBM) if spec is HBM else value
        for value, spec in zip(inputs, specs)
    ]
    return pl.pallas_call(
        kernel,
        out_shape=out,
        in_specs=specs,
        out_specs=jax.tree.map(lambda _: VMEM, out),
        scratch_shapes=list(scratch),
        cost_estimate=pl.CostEstimate(flops=flops, bytes_accessed=moved, transcendentals=0),
        compiler_params=pltpu.CompilerParams(vmem_limit_bytes=16 << 20),
        name=name,
    )(*inputs)


def split(value):
    high = value.astype(BF16)
    low = (value - high.astype(F32)).astype(BF16)
    return high, low


def join(ref, at, width):
    high = ref[:, at : at + width].astype(F32)
    return high + ref[:, at + width : at + 2 * width].astype(F32)


def fetch(sources, targets, sems):
    copies = [
        pltpu.make_async_copy(source, target, sems.at[index])
        for index, (source, target) in enumerate(zip(sources, targets))
    ]
    for copy in copies:
        copy.start()
    return copies


def first_kernel(grad_hbm, basis_hbm, out_ref, grad_ref, basis_ref, sems):
    rank, rows = basis_ref.shape
    copies = fetch((grad_hbm, basis_hbm), (grad_ref, basis_ref), sems)
    copies[0].wait()
    rounded = grad_ref[...].astype(BF16)
    out_ref[:, :rows] = rounded
    copies[1].wait()
    partial = lax.dot_general(rounded, basis_ref[...], NT, preferred_element_type=F32)
    high, low = split(partial)
    out_ref[:, rows : rows + rank] = high
    out_ref[:, rows + rank :] = low


def table_kernel(*refs):
    inputs, (mix_ref, flag_ref), held, sems = refs[:5], refs[5:7], refs[7:12], refs[12]
    count_ref, offset_ref, source_ref, far_ref, cores_ref = held
    owner = lax.axis_index("cell")
    slots, rank, _ = cores_ref.shape
    for copy in fetch(inputs, held, sems):
        copy.wait()
    cells = mix_ref.shape[1] // rank
    used = far_ref[owner]
    for step in range(cells):
        total = jnp.zeros((rank, rank), F32)
        for slot in range(slots):
            hit = jnp.logical_and(source_ref[owner, slot] == (owner ^ step), slot < used)
            total = total + jnp.where(hit, cores_ref[slot], 0.0)
        mix_ref[:, step * rank : (step + 1) * rank] = total
    beyond = owner ^ 2
    asked = beyond + offset_ref[beyond] == owner ^ 1
    beside = offset_ref[owner] + owner == owner ^ 1
    double = count_ref[owner] == 2
    for row, value in enumerate((asked, beside, double)):
        flag_ref[row] = jnp.full(flag_ref.shape[1:], value.astype(F32), F32)


def pick(flag_ref, row, yes, no):
    shape = yes.shape
    mask = jnp.broadcast_to(flag_ref[row][:1, :1], shape) > 0.5
    return jnp.where(mask, yes.astype(F32), no.astype(F32)).astype(BF16)


def second_kernel(flag_ref, mine_ref, near_ref, out_ref, *, rows):
    out_ref[:, :rows] = pick(flag_ref, 0, near_ref[:, :rows], mine_ref[:, :rows])
    tail = mine_ref.shape[1] - rows
    out_ref[:, rows : rows + tail] = mine_ref[:, rows:]
    out_ref[:, rows + tail :] = near_ref[:, rows:]


def third_kernel(flag_ref, mix_ref, mine_ref, near_ref, far_ref, out_ref, *, rows):
    rank = mix_ref.shape[0]
    beside = pick(flag_ref, 1, near_ref[:, :rows], far_ref[:, :rows])
    beside = pick(flag_ref, 2, beside, jnp.zeros_like(beside))
    out_ref[:, :rows] = mine_ref[:, :rows]
    out_ref[:, rows : 2 * rows] = beside
    table = jnp.concatenate(
        (
            join(mine_ref, rows, rank),
            join(near_ref, rows, rank),
            join(far_ref, rows, rank),
            join(far_ref, rows + 2 * rank, rank),
        ),
        axis=1,
    )
    core = lax.dot_general(
        table, mix_ref[...], NT, precision=lax.Precision.HIGHEST, preferred_element_type=F32
    )
    high, low = split(core)
    out_ref[:, 2 * rows : 2 * rows + rank] = high
    out_ref[:, 2 * rows + rank :] = low


def widen_kernel(after_ref, mine_ref, other_ref, out_ref, *, rank):
    del after_ref
    body = mine_ref.shape[1] - 2 * rank
    out_ref[:, :body] = mine_ref[:, :body]
    out_ref[:, body : 2 * body] = other_ref[:, :body]
    high, low = split(join(mine_ref, body, rank) + join(other_ref, body, rank))
    out_ref[:, 2 * body : 2 * body + rank] = high
    out_ref[:, 2 * body + rank :] = low


def stage_kernel(after_ref, tiles_hbm, basis_hbm, tiles_ref, basis_ref, sems):
    del after_ref
    parts = tiles_ref.shape[0]
    sources = [tiles_hbm.at[part] for part in range(parts)] + [basis_hbm]
    targets = [tiles_ref.at[part] for part in range(parts)] + [basis_ref]
    for copy in fetch(sources, targets, sems):
        copy.wait()


def near(total, held_ref, tiles_ref, order):
    place = lax.axis_index("col")
    rows = tiles_ref.shape[1]
    for item, (part, spot) in enumerate(order):
        columns = pl.ds(pl.multiple_of((place ^ spot) * rows, rows), rows)
        total = total + lax.dot_general(
            held_ref[:, item * rows : (item + 1) * rows],
            tiles_ref[part, :, columns],
            NT,
            preferred_element_type=F32,
        )
    return total


def near_kernel(mine_ref, tiles_ref, out_ref, *, order):
    out_ref[...] = near(jnp.zeros(out_ref.shape, F32), mine_ref, tiles_ref, order)


def last_kernel(sum_ref, mine_ref, other_ref, basis_ref, tiles_ref, out_ref, *, order):
    rank = basis_ref.shape[0]
    body = mine_ref.shape[1] - 2 * rank
    core = join(mine_ref, body, rank) + join(other_ref, body, rank)
    far = jnp.dot(core.astype(BF16), basis_ref[...], preferred_element_type=F32)
    out_ref[...] = near(sum_ref[...] + far, other_ref, tiles_ref, order)


def swap(value, axis, step):
    size = lax.axis_size(axis)
    return lax.ppermute(value, axis, [(i, i ^ step) for i in range(size)])


def shifted(value, axis, by):
    size = lax.axis_size(axis)
    return lax.ppermute(value, axis, [(i, i + by) for i in range(size) if 0 <= i + by < size])


def over_small_chain(first, tables, cores, rows):
    width, length = first.shape
    rank = cores.shape[1]
    beyond = swap(first, "cell", 1)
    mix, flags = call(
        table_kernel,
        (
            jax.ShapeDtypeStruct((rank, 4 * rank), F32),
            jax.ShapeDtypeStruct((3, 8, 128), F32),
        ),
        (*tables, cores),
        [HBM] * 5,
        scratch=[
            *(pltpu.SMEM(table.shape, table.dtype) for table in tables),
            pltpu.VMEM(cores.shape, cores.dtype),
            pltpu.SemaphoreType.DMA((5,)),
        ],
        moved=cores.size * 4,
        name="tables",
    )
    second = call(
        functools.partial(second_kernel, rows=rows),
        jax.ShapeDtypeStruct((width, 2 * length - rows), BF16),
        (flags, first, beyond),
        [VMEM] * 3,
        moved=4 * first.size,
        name="second",
    )
    far = swap(second, "cell", 2)
    return call(
        functools.partial(third_kernel, rows=rows),
        jax.ShapeDtypeStruct((width, length + rows), BF16),
        (flags, mix, first, beyond, far),
        [VMEM] * 5,
        moved=8 * first.size,
        name="third",
    )


def over_long_chain(first, tables, cores, rows):
    owner = lax.axis_index("cell")
    rank = cores.shape[1]
    counts, offsets, sources, used = (table[owner] for table in tables)
    steps = [step for step in range(-REACH, REACH + 1) if step]
    moved = jnp.stack([shifted(first[:, :rows], "cell", -step) for step in steps])
    beside = lax.dynamic_index_in_dim(
        moved, offsets + REACH - (offsets > 0).astype(jnp.int32), 0, keepdims=False
    )
    beside = jnp.where(counts == 2, beside, jnp.zeros_like(beside))
    high, low = first[:, rows : rows + rank], first[:, rows + rank :]
    partial = high.astype(F32) + low.astype(F32)
    table = lax.all_gather(partial[None], "cell", axis=0, tiled=True)
    picked = jnp.take(table, sources, axis=0)
    slots = jnp.arange(cores.shape[0], dtype=jnp.int32)
    masked = jnp.where((slots < used)[:, None, None], cores, jnp.zeros_like(cores))
    core = jnp.einsum("kab,kwb->wa", masked, picked, precision=lax.Precision.HIGHEST)
    return jnp.concatenate((first[:, :rows], beside, *split(core)), axis=1)


def body(
    grad, near_tiles, tile_count, near_offset, far_src, far_count, far_cores, basis_out, basis_in
):
    rows, width = grad.shape
    rank = basis_in.shape[1]
    cells, parts = lax.axis_size("cell"), lax.axis_size("col")
    first = call(
        first_kernel,
        jax.ShapeDtypeStruct((width, rows + 2 * rank), BF16),
        (grad.T, basis_in.T),
        [HBM] * 2,
        scratch=[
            pltpu.VMEM((width, rows), grad.dtype),
            pltpu.VMEM((rank, rows), basis_in.dtype),
            pltpu.SemaphoreType.DMA((2,)),
        ],
        moved=8 * grad.size,
        name="first",
    )
    tables = (tile_count, near_offset, far_src, far_count)
    over_cells = over_small_chain if cells == 2 * REACH else over_long_chain
    held = over_cells(first, tables, far_cores[0], rows)
    tiles, basis = call(
        stage_kernel,
        (
            jax.ShapeDtypeStruct(near_tiles.shape[1:], near_tiles.dtype),
            jax.ShapeDtypeStruct((rank, rows), basis_out.dtype),
        ),
        (held, near_tiles[0], basis_out.T),
        [VMEM, HBM, HBM],
        scratch=[pltpu.SemaphoreType.DMA((near_tiles.shape[1] + 1,))],
        moved=2 * near_tiles.size,
        name="stage",
    )
    order = [(0, 0), (1, 0)]
    step = parts // 2
    while step > 1:
        other = swap(held, "col", step)
        held = call(
            functools.partial(widen_kernel, rank=rank),
            jax.ShapeDtypeStruct((width, 2 * held.shape[1] - 2 * rank), BF16),
            (basis, held, other),
            [VMEM] * 3,
            moved=8 * held.size,
            name="widen",
        )
        order += [(part, spot ^ step) for part, spot in order]
        step //= 2
    other = swap(held, "col", 1)
    total = call(
        functools.partial(near_kernel, order=order),
        jax.ShapeDtypeStruct((width, rows), F32),
        (held, tiles),
        [VMEM] * 2,
        flops=tiles.size * width,
        moved=tiles.size,
        name="near",
    )
    out = call(
        functools.partial(last_kernel, order=[(part, spot ^ 1) for part, spot in order]),
        jax.ShapeDtypeStruct((width, rows), F32),
        (total, held, other, basis, tiles),
        [VMEM] * 5,
        flops=tiles.size * width,
        moved=tiles.size,
        name="last",
    )
    return out.T


def solution(mesh):
    placed = (
        P(("chain", "cell", "col"), None),
        P("cell", None, "col", None),
        P(),
        P(),
        P(),
        P(),
        P("cell", None, None, None),
        P(("cell", "col"), None),
        P(("cell", "col"), None),
    )
    return jax.shard_map(
        body,
        mesh=mesh,
        in_specs=placed,
        out_specs=P(("chain", "cell", "col"), None),
        check_vma=False,
    )
```

```python
import functools

import jax
import jax.numpy as jnp
from jax import lax
from jax.experimental import pallas as pl
from jax.experimental.pallas import tpu as pltpu
from jax.sharding import PartitionSpec as P


REACH = 2
F32 = jnp.float32
BF16 = jnp.bfloat16
VMEM = pl.BlockSpec(memory_space=pltpu.VMEM)
HBM = pl.BlockSpec(memory_space=pltpu.HBM)
NT = (((1,), (1,)), ((), ()))


def call(kernel, out, inputs, specs, home=VMEM, scratch=(), flops=0, moved=0):
    inputs = [
        pltpu.with_memory_space_constraint(value, pltpu.HBM) if spec is HBM else value
        for value, spec in zip(inputs, specs)
    ]
    return pl.pallas_call(
        kernel,
        out_shape=out,
        in_specs=specs,
        out_specs=jax.tree.map(lambda _: home, out),
        scratch_shapes=list(scratch),
        cost_estimate=pl.CostEstimate(flops=flops, bytes_accessed=moved, transcendentals=0),
        compiler_params=pltpu.CompilerParams(vmem_limit_bytes=16 << 20),
    )(*inputs)


def pieces(value, count=3):
    out = []
    for _ in range(count):
        out.append(value.astype(BF16))
        value = value - out[-1].astype(F32)
    return out


def split(value):
    return pieces(value, 2)


def mixed(tail, mix_ref, at):
    total = None
    for piece in range(mix_ref.shape[0]):
        part = lax.dot_general(
            tail, mix_ref[piece, :, at : at + tail.shape[1]], NT, preferred_element_type=F32
        )
        total = part if total is None else total + part
    return total


def join(ref, at, width):
    high = ref[:, at : at + width].astype(F32)
    return high + ref[:, at + width : at + 2 * width].astype(F32)


def fetch(sources, targets, sems):
    copies = [
        pltpu.make_async_copy(source, target, sems.at[index])
        for index, (source, target) in enumerate(zip(sources, targets))
    ]
    for copy in copies:
        copy.start()
    return copies


def first_kernel(grad_hbm, basis_hbm, out_ref, own_ref, grad_ref, basis_ref, sems):
    rank, rows = basis_ref.shape
    copies = fetch((grad_hbm, basis_hbm), (grad_ref, basis_ref), sems)
    copies[0].wait()
    rounded = grad_ref[...].astype(BF16)
    out_ref[:, :rows] = rounded
    own_ref[...] = rounded
    copies[1].wait()
    partial = lax.dot_general(rounded, basis_ref[...], NT, preferred_element_type=F32)
    high, low = split(partial)
    out_ref[:, rows : rows + rank] = high
    out_ref[:, rows + rank :] = low


def table_kernel(*refs):
    tiles_hbm, inputs, (mix_ref, flag_ref, tiles_ref) = refs[0], refs[1:6], refs[6:9]
    held, sems = refs[9:14], refs[14]
    count_ref, offset_ref, source_ref, far_ref, cores_ref = held
    owner = lax.axis_index("cell")
    slots, rank, _ = cores_ref.shape
    copies = fetch((*inputs, tiles_hbm.at[0]), (*held, tiles_ref), sems)
    for copy in copies[:-1]:
        copy.wait()
    cells = mix_ref.shape[2] // (2 * rank)
    used = far_ref[owner]
    for step in range(cells):
        total = jnp.zeros((rank, rank), F32)
        for slot in range(slots):
            hit = jnp.logical_and(source_ref[owner, slot] == (owner ^ step), slot < used)
            total = total + jnp.where(hit, cores_ref[slot], 0.0)
        for piece, value in enumerate(pieces(total)):
            for twin in range(2):
                at = (2 * step + twin) * rank
                mix_ref[piece, :, at : at + rank] = value
    beyond = owner ^ 2
    asked = beyond + offset_ref[beyond] == owner ^ 1
    beside = offset_ref[owner] + owner == owner ^ 1
    double = count_ref[owner] == 2
    for row, value in enumerate((asked, beside, double)):
        flag_ref[row] = jnp.full(flag_ref.shape[1:], value.astype(F32), F32)
    copies[-1].wait()


def pick(flag_ref, row, yes, no):
    shape = yes.shape
    mask = jnp.broadcast_to(flag_ref[row][:1, :1], shape) > 0.5
    return jnp.where(mask, yes.astype(F32), no.astype(F32)).astype(BF16)


def second_kernel(flag_ref, mine_ref, near_ref, out_ref, *, rows):
    out_ref[:, :rows] = pick(flag_ref, 0, near_ref[:, :rows], mine_ref[:, :rows])
    tail = mine_ref.shape[1] - rows
    out_ref[:, rows : rows + tail] = mine_ref[:, rows:]
    out_ref[:, rows + tail :] = near_ref[:, rows:]


def early_kernel(mix_ref, mine_ref, near_ref, after_ref, out_ref, *, rows):
    del after_ref
    tail = mine_ref.shape[1] - rows
    core = mixed(mine_ref[:, rows:], mix_ref, 0)
    out_ref[...] = core + mixed(near_ref[:, rows:], mix_ref, tail)


def third_kernel(flag_ref, mix_ref, core_ref, near_ref, far_ref, out_ref, *, rows):
    rank = core_ref.shape[1]
    beside = pick(flag_ref, 1, near_ref[:, :rows], far_ref[:, :rows])
    out_ref[:, :rows] = pick(flag_ref, 2, beside, jnp.zeros_like(beside))
    tail = near_ref.shape[1] - rows
    high, low = split(core_ref[...] + mixed(far_ref[:, rows:], mix_ref, 2 * tail))
    out_ref[:, rows : rows + rank] = high
    out_ref[:, rows + rank :] = low


def widen_kernel(mine_ref, other_ref, out_ref, *, rows):
    rank = (mine_ref.shape[1] - rows) // 2
    out_ref[:, :rows] = other_ref[:, :rows]
    high, low = split(join(mine_ref, rows, rank) + join(other_ref, rows, rank))
    out_ref[:, rows : rows + rank] = high
    out_ref[:, rows + rank :] = low


def stage_kernel(tiles_hbm, tiles_ref, sems):
    for copy in fetch((tiles_hbm.at[0],), (tiles_ref,), sems):
        copy.wait()


def numbered(order, step=0):
    return [(item, part, spot ^ step) for item, (part, spot) in enumerate(order)]


def near(total, held_ref, tiles, order):
    place = lax.axis_index("col")
    rows = tiles[0].shape[0]
    for item, part, spot in order:
        columns = pl.ds(pl.multiple_of((place ^ spot) * rows, rows), rows)
        total = total + lax.dot_general(
            held_ref[:, item * rows : (item + 1) * rows],
            tiles[part][:, columns],
            NT,
            preferred_element_type=F32,
        )
    return total


def early_near_kernel(
    held_ref, own_ref, tiles_hbm, basis_hbm, out_ref, tiles_ref, basis_ref, sems, *, order
):
    copies = fetch((tiles_hbm.at[1], basis_hbm), (tiles_ref, basis_ref), sems)
    tiles = (own_ref, tiles_ref)
    ready = [entry for entry in order if entry[1] == 0]
    total = near(jnp.zeros(out_ref.shape, F32), held_ref, tiles, ready)
    for copy in copies:
        copy.wait()
    out_ref[...] = near(total, held_ref, tiles, [entry for entry in order if entry[1] == 1])


def near_kernel(sum_ref, early_ref, late_ref, own_ref, tiles_ref, out_ref, *, early, late):
    tiles = (own_ref, tiles_ref)
    out_ref[...] = near(near(sum_ref[...], late_ref, tiles, late), early_ref, tiles, early)


def last_kernel(
    sum_ref, mine_ref, other_ref, basis_ref, own_ref, tiles_ref, out_ref, *, order
):
    rank, rows = basis_ref.shape
    core = (join(mine_ref, rows, rank) + join(other_ref, rows, rank)).astype(BF16)
    far = jnp.dot(core, basis_ref[...], preferred_element_type=F32)
    out_ref[...] = near(sum_ref[...] + far, other_ref, (own_ref, tiles_ref), order)


def swap(value, axis, step):
    size = lax.axis_size(axis)
    return lax.ppermute(value, axis, [(i, i ^ step) for i in range(size)])


def shifted(value, axis, by):
    size = lax.axis_size(axis)
    return lax.ppermute(value, axis, [(i, i + by) for i in range(size) if 0 <= i + by < size])


def over_small_chain(first, tables, cores, tiles):
    width, length = first.shape
    rows, rank = tiles.shape[1], cores.shape[1]
    beyond = swap(first, "cell", 1)
    mix, flags, own_tile = call(
        table_kernel,
        (
            jax.ShapeDtypeStruct((3, rank, 8 * rank), BF16),
            jax.ShapeDtypeStruct((3, 8, 128), F32),
            jax.ShapeDtypeStruct(tiles.shape[1:], tiles.dtype),
        ),
        (tiles, *tables, cores),
        [HBM] * 6,
        scratch=[
            *(pltpu.SMEM(table.shape, table.dtype) for table in tables),
            pltpu.VMEM(cores.shape, cores.dtype),
            pltpu.SemaphoreType.DMA((6,)),
        ],
        moved=cores.size * 4 + tiles.size,
    )
    second = call(
        functools.partial(second_kernel, rows=rows),
        jax.ShapeDtypeStruct((width, 2 * length - rows), BF16),
        (flags, first, beyond),
        [VMEM] * 3,
        moved=4 * first.size,
    )
    far = swap(second, "cell", 2)
    core = call(
        functools.partial(early_kernel, rows=rows),
        jax.ShapeDtypeStruct((width, rank), F32),
        (mix, first, beyond, second),
        [VMEM] * 4,
        moved=8 * first.size,
    )
    third = call(
        functools.partial(third_kernel, rows=rows),
        jax.ShapeDtypeStruct((width, length), BF16),
        (flags, mix, core, beyond, far),
        [VMEM] * 5,
        moved=8 * first.size,
    )
    return third, own_tile


def over_long_chain(first, tables, cores, tiles):
    owner = lax.axis_index("cell")
    rows, rank = tiles.shape[1], cores.shape[1]
    own_tile = call(
        stage_kernel,
        jax.ShapeDtypeStruct(tiles.shape[1:], tiles.dtype),
        (tiles,),
        [HBM],
        scratch=[pltpu.SemaphoreType.DMA((1,))],
        moved=tiles.size,
    )
    counts, offsets, sources, used = (table[owner] for table in tables)
    steps = [step for step in range(-REACH, REACH + 1) if step]
    moved = jnp.stack([shifted(first[:, :rows], "cell", -step) for step in steps])
    beside = lax.dynamic_index_in_dim(
        moved, offsets + REACH - (offsets > 0).astype(jnp.int32), 0, keepdims=False
    )
    beside = jnp.where(counts == 2, beside, jnp.zeros_like(beside))
    high, low = first[:, rows : rows + rank], first[:, rows + rank :]
    partial = high.astype(F32) + low.astype(F32)
    table = lax.all_gather(partial[None], "cell", axis=0, tiled=True)
    picked = jnp.take(table, sources, axis=0)
    slots = jnp.arange(cores.shape[0], dtype=jnp.int32)
    masked = jnp.where((slots < used)[:, None, None], cores, jnp.zeros_like(cores))
    core = jnp.einsum("kab,kwb->wa", masked, picked, precision=lax.Precision.HIGHEST)
    return jnp.concatenate((beside, *split(core)), axis=1), own_tile


def body(
    grad, near_tiles, tile_count, near_offset, far_src, far_count, far_cores, basis_out, basis_in
):
    rows, width = grad.shape
    rank = basis_in.shape[1]
    cells, parts = lax.axis_size("cell"), lax.axis_size("col")
    first, own = call(
        first_kernel,
        (
            jax.ShapeDtypeStruct((width, rows + 2 * rank), BF16),
            jax.ShapeDtypeStruct((width, rows), BF16),
        ),
        (grad.T, basis_in.T),
        [HBM] * 2,
        scratch=[
            pltpu.VMEM((width, rows), grad.dtype),
            pltpu.VMEM((rank, rows), basis_in.dtype),
            pltpu.SemaphoreType.DMA((2,)),
        ],
        moved=8 * grad.size,
    )
    tables = (tile_count, near_offset, far_src, far_count)
    tiles = near_tiles[0]
    over_cells = over_small_chain if cells == 2 * REACH else over_long_chain
    late, own_tile = over_cells(first, tables, far_cores[0], tiles)
    late_order = [(1, 0)]
    early, early_order = own, [(0, 0)]
    steps = [1 << bit for bit in reversed(range(parts.bit_length() - 1))]
    for step in steps:
        early_other = swap(early, "col", step)
        late_other = swap(late, "col", step)
        across = [(part, spot ^ step) for part, spot in early_order]
        if step > 1:
            early = jnp.concatenate((early, early_other, late[:, :rows]), axis=1)
            early_order = early_order + across + late_order
            late_order = [(part, spot ^ step) for part, spot in late_order]
            late = call(
                functools.partial(widen_kernel, rows=rows),
                jax.ShapeDtypeStruct(late.shape, BF16),
                (late, late_other),
                [VMEM] * 2,
                moved=8 * late.size,
            )
    total, other_tile, basis = call(
        functools.partial(early_near_kernel, order=numbered(early_order)),
        (
            jax.ShapeDtypeStruct((width, rows), F32),
            jax.ShapeDtypeStruct(tiles.shape[1:], tiles.dtype),
            jax.ShapeDtypeStruct((rank, rows), basis_out.dtype),
        ),
        (early, own_tile, tiles, basis_out.T),
        [VMEM, VMEM, HBM, HBM],
        scratch=[pltpu.SemaphoreType.DMA((2,))],
        flops=tiles.size * width,
        moved=tiles.size,
    )
    total = call(
        functools.partial(near_kernel, early=numbered(across), late=numbered(late_order)),
        jax.ShapeDtypeStruct((width, rows), F32),
        (total, early_other, late, own_tile, other_tile),
        [VMEM] * 5,
        flops=tiles.size * width,
        moved=tiles.size,
    )
    out = call(
        functools.partial(last_kernel, order=numbered(late_order, 1)),
        jax.ShapeDtypeStruct((width, rows), F32),
        (total, late, late_other, basis, own_tile, other_tile),
        [VMEM] * 6,
        flops=tiles.size * width,
        moved=tiles.size,
    )
    return out.T


def solution(mesh):
    placed = (
        P(("chain", "cell", "col"), None),
        P("cell", None, "col", None),
        P(),
        P(),
        P(),
        P(),
        P("cell", None, None, None),
        P(("cell", "col"), None),
        P(("cell", "col"), None),
    )

    return jax.shard_map(
        body,
        mesh=mesh,
        in_specs=placed,
        out_specs=P(("chain", "cell", "col"), None),
        check_vma=False,
    )
```

```python
import functools

import jax
import jax.numpy as jnp
from jax import lax
from jax.experimental import pallas as pl
from jax.experimental.pallas import tpu as pltpu
from jax.sharding import PartitionSpec as P


REACH = 2
F32 = jnp.float32
BF16 = jnp.bfloat16
VMEM = pl.BlockSpec(memory_space=pltpu.VMEM)
HBM = pl.BlockSpec(memory_space=pltpu.HBM)
NT = (((1,), (1,)), ((), ()))


def call(kernel, out, inputs, specs, home=VMEM, scratch=(), flops=0, moved=0):
    inputs = [
        pltpu.with_memory_space_constraint(value, pltpu.HBM) if spec is HBM else value
        for value, spec in zip(inputs, specs)
    ]
    return pl.pallas_call(
        kernel,
        out_shape=out,
        in_specs=specs,
        out_specs=jax.tree.map(lambda _: home, out),
        scratch_shapes=list(scratch),
        cost_estimate=pl.CostEstimate(flops=flops, bytes_accessed=moved, transcendentals=0),
        compiler_params=pltpu.CompilerParams(vmem_limit_bytes=16 << 20),
    )(*inputs)


def pieces(value, count=3):
    out = []
    for _ in range(count):
        out.append(value.astype(BF16))
        value = value - out[-1].astype(F32)
    return out


def split(value):
    return pieces(value, 2)


def mixed(tail, mix_ref, at):
    total = None
    for piece in range(mix_ref.shape[0]):
        part = lax.dot_general(
            tail, mix_ref[piece, :, at : at + tail.shape[1]], NT, preferred_element_type=F32
        )
        total = part if total is None else total + part
    return total


def join(ref, at, width):
    high = ref[:, at : at + width].astype(F32)
    return high + ref[:, at + width : at + 2 * width].astype(F32)


def fetch(sources, targets, sems):
    copies = [
        pltpu.make_async_copy(source, target, sems.at[index])
        for index, (source, target) in enumerate(zip(sources, targets))
    ]
    for copy in copies:
        copy.start()
    return copies


def first_kernel(grad_hbm, basis_hbm, out_ref, own_ref, grad_ref, basis_ref, sems):
    rank, rows = basis_ref.shape
    copies = fetch((grad_hbm, basis_hbm), (grad_ref, basis_ref), sems)
    copies[0].wait()
    rounded = grad_ref[...].astype(BF16)
    out_ref[:, :rows] = rounded
    own_ref[...] = rounded
    copies[1].wait()
    partial = lax.dot_general(rounded, basis_ref[...], NT, preferred_element_type=F32)
    high, low = split(partial)
    out_ref[:, rows : rows + rank] = high
    out_ref[:, rows + rank :] = low


def table_kernel(*refs):
    tiles_hbm, inputs, (mix_ref, flag_ref, tiles_ref) = refs[0], refs[1:6], refs[6:9]
    held, sems = refs[9:14], refs[14]
    count_ref, offset_ref, source_ref, far_ref, cores_ref = held
    owner = lax.axis_index("cell")
    slots, rank, _ = cores_ref.shape
    copies = fetch((*inputs, tiles_hbm.at[0]), (*held, tiles_ref), sems)
    for copy in copies[:-1]:
        copy.wait()
    cells = mix_ref.shape[2] // (2 * rank)
    used = far_ref[owner]
    place = lax.axis_index("col")
    steps = [cell_step(place, stage) for stage in range(2)]
    for step in range(cells):
        total = jnp.zeros((rank, rank), F32)
        source = owner ^ (steps[0] * (step & 1)) ^ (steps[1] * (step >> 1))
        for slot in range(slots):
            hit = jnp.logical_and(source_ref[owner, slot] == source, slot < used)
            total = total + jnp.where(hit, cores_ref[slot], 0.0)
        for piece, value in enumerate(pieces(total)):
            for twin in range(2):
                at = (2 * step + twin) * rank
                mix_ref[piece, :, at : at + rank] = value
    beyond = owner ^ steps[1]
    asked = beyond + offset_ref[beyond] == owner ^ steps[0]
    beside = offset_ref[owner] + owner == owner ^ steps[0]
    double = count_ref[owner] == 2
    for row, value in enumerate((asked, beside, double)):
        flag_ref[row] = jnp.full(flag_ref.shape[1:], value.astype(F32), F32)
    copies[-1].wait()


def pick(flag_ref, row, yes, no, use=None):
    mask = jnp.broadcast_to(flag_ref[row][:1, :1], yes.shape) > 0.5
    value = jnp.where(mask, yes.astype(F32), no.astype(F32))
    if use is not None:
        value = jnp.where(use > 0.5, value, 0.0)
    return value.astype(BF16)


def second_kernel(flag_ref, mine_ref, near_ref, out_ref, *, rows):
    out_ref[:, :rows] = pick(flag_ref, 0, near_ref[:, :rows], mine_ref[:, :rows])
    tail = mine_ref.shape[1] - rows
    out_ref[:, rows : rows + tail] = mine_ref[:, rows:]
    out_ref[:, rows + tail :] = near_ref[:, rows:]


def early_kernel(mix_ref, mine_ref, near_ref, after_ref, out_ref, *, rows):
    del after_ref
    tail = mine_ref.shape[1] - rows
    core = mixed(mine_ref[:, rows:], mix_ref, 0)
    out_ref[...] = core + mixed(near_ref[:, rows:], mix_ref, tail)


def third_kernel(flag_ref, mix_ref, core_ref, near_ref, far_ref, out_ref, *, rows):
    rank = core_ref.shape[1]
    use = jnp.broadcast_to(flag_ref[2][:1, :1], (far_ref.shape[0], rows))
    out_ref[:, :rows] = pick(flag_ref, 1, near_ref[:, :rows], far_ref[:, :rows], use)
    tail = near_ref.shape[1] - rows
    high, low = split(core_ref[...] + mixed(far_ref[:, rows:], mix_ref, 2 * tail))
    out_ref[:, rows : rows + rank] = high
    out_ref[:, rows + rank :] = low


def stage_kernel(tiles_hbm, tiles_ref, sems):
    for copy in fetch((tiles_hbm.at[0],), (tiles_ref,), sems):
        copy.wait()


def flipped(items, step, at=0):
    return [(lane + at, part, spot ^ step) for lane, part, spot in items]


def near(total, held_ref, tiles, order):
    place = lax.axis_index("col")
    rows = tiles[0].shape[0]
    for lane, part, spot in order:
        columns = pl.ds(pl.multiple_of((place ^ spot) * rows, rows), rows)
        total = total + lax.dot_general(
            held_ref[:, lane : lane + rows],
            tiles[part][:, columns],
            NT,
            preferred_element_type=F32,
        )
    return total


def early_near_kernel(
    held_ref, own_ref, tiles_hbm, basis_hbm, out_ref, tiles_ref, basis_ref, sems, *, order
):
    copies = fetch((tiles_hbm.at[1], basis_hbm), (tiles_ref, basis_ref), sems)
    tiles = (own_ref, tiles_ref)
    ready = [entry for entry in order if entry[1] == 0]
    total = near(jnp.zeros(out_ref.shape, F32), held_ref, tiles, ready)
    for copy in copies:
        copy.wait()
    out_ref[...] = near(total, held_ref, tiles, [entry for entry in order if entry[1] == 1])


def near_kernel(
    sum_ref, mine_ref, early_ref, late_ref, own_ref, tiles_ref, out_ref, core_ref, *, early, late, cores
):
    tiles = (own_ref, tiles_ref)
    out_ref[...] = near(near(sum_ref[...], late_ref, tiles, late), early_ref, tiles, early)
    core = jnp.zeros(core_ref.shape, F32)
    for ref, lanes in zip((mine_ref, early_ref, late_ref), cores):
        for lane in lanes:
            core = core + join(ref, lane, core.shape[1])
    core_ref[...] = core


def last_kernel(
    sum_ref, core_ref, other_ref, basis_ref, own_ref, tiles_ref, out_ref, *, late, lane
):
    core = (core_ref[...] + join(other_ref, lane, core_ref.shape[1])).astype(BF16)
    far = jnp.dot(core, basis_ref[...], preferred_element_type=F32)
    out_ref[...] = near(sum_ref[...] + far, other_ref, (own_ref, tiles_ref), late)


def swap(value, axis, step):
    size = lax.axis_size(axis)
    return lax.ppermute(value, axis, [(i, i ^ step) for i in range(size)])


def cell_step(place, stage):
    return 1 + (place + stage + 1) % 2


def crossed(value, stage):
    cells, parts = lax.axis_size("cell"), lax.axis_size("col")
    pairs = [
        (cell * parts + place, (cell ^ cell_step(place, stage)) * parts + place)
        for cell in range(cells)
        for place in range(parts)
    ]
    return lax.ppermute(value, ("cell", "col"), pairs)


def shifted(value, axis, by):
    size = lax.axis_size(axis)
    return lax.ppermute(value, axis, [(i, i + by) for i in range(size) if 0 <= i + by < size])


def over_small_chain(first, tables, cores, tiles):
    width, length = first.shape
    rows, rank = tiles.shape[1], cores.shape[1]
    beyond = crossed(first, 0)
    mix, flags, own_tile = call(
        table_kernel,
        (
            jax.ShapeDtypeStruct((3, rank, 8 * rank), BF16),
            jax.ShapeDtypeStruct((3, 8, 128), F32),
            jax.ShapeDtypeStruct(tiles.shape[1:], tiles.dtype),
        ),
        (tiles, *tables, cores),
        [HBM] * 6,
        scratch=[
            *(pltpu.SMEM(table.shape, table.dtype) for table in tables),
            pltpu.VMEM(cores.shape, cores.dtype),
            pltpu.SemaphoreType.DMA((6,)),
        ],
        moved=cores.size * 4 + tiles.size,
    )
    second = call(
        functools.partial(second_kernel, rows=rows),
        jax.ShapeDtypeStruct((width, 2 * length - rows), BF16),
        (flags, first, beyond),
        [VMEM] * 3,
        moved=4 * first.size,
    )
    far = crossed(second, 1)
    core = call(
        functools.partial(early_kernel, rows=rows),
        jax.ShapeDtypeStruct((width, rank), F32),
        (mix, first, beyond, second),
        [VMEM] * 4,
        moved=8 * first.size,
    )
    third = call(
        functools.partial(third_kernel, rows=rows),
        jax.ShapeDtypeStruct((width, length), BF16),
        (flags, mix, core, beyond, far),
        [VMEM] * 5,
        moved=8 * first.size,
    )
    return third, own_tile


def over_long_chain(first, tables, cores, tiles):
    owner = lax.axis_index("cell")
    rows, rank = tiles.shape[1], cores.shape[1]
    own_tile = call(
        stage_kernel,
        jax.ShapeDtypeStruct(tiles.shape[1:], tiles.dtype),
        (tiles,),
        [HBM],
        scratch=[pltpu.SemaphoreType.DMA((1,))],
        moved=tiles.size,
    )
    counts, offsets, sources, used = (table[owner] for table in tables)
    steps = [step for step in range(-REACH, REACH + 1) if step]
    moved = jnp.stack([shifted(first[:, :rows], "cell", -step) for step in steps])
    beside = lax.dynamic_index_in_dim(
        moved, offsets + REACH - (offsets > 0).astype(jnp.int32), 0, keepdims=False
    )
    beside = jnp.where(counts == 2, beside, jnp.zeros_like(beside))
    high, low = first[:, rows : rows + rank], first[:, rows + rank :]
    partial = high.astype(F32) + low.astype(F32)
    table = lax.all_gather(partial[None], "cell", axis=0, tiled=True)
    picked = jnp.take(table, sources, axis=0)
    slots = jnp.arange(cores.shape[0], dtype=jnp.int32)
    masked = jnp.where((slots < used)[:, None, None], cores, jnp.zeros_like(cores))
    core = jnp.einsum("kab,kwb->wa", masked, picked, precision=lax.Precision.HIGHEST)
    return jnp.concatenate((beside, *split(core)), axis=1), own_tile


def body(
    grad, near_tiles, tile_count, near_offset, far_src, far_count, far_cores, basis_out, basis_in
):
    rows, width = grad.shape
    rank = basis_in.shape[1]
    cells, parts = lax.axis_size("cell"), lax.axis_size("col")
    first, own = call(
        first_kernel,
        (
            jax.ShapeDtypeStruct((width, rows + 2 * rank), BF16),
            jax.ShapeDtypeStruct((width, rows), BF16),
        ),
        (grad.T, basis_in.T),
        [HBM] * 2,
        scratch=[
            pltpu.VMEM((width, rows), grad.dtype),
            pltpu.VMEM((rank, rows), basis_in.dtype),
            pltpu.SemaphoreType.DMA((2,)),
        ],
        moved=8 * grad.size,
    )
    tables = (tile_count, near_offset, far_src, far_count)
    tiles = near_tiles[0]
    over_cells = over_small_chain if cells == 2 * REACH else over_long_chain
    late, own_tile = over_cells(first, tables, far_cores[0], tiles)
    late_items, early_items = [(0, 1, 0)], [(0, 0, 0)]
    early, early_cores = own, []
    steps = [1 << bit for bit in reversed(range(parts.bit_length() - 1))]
    for step in steps:
        early_other = swap(early, "col", step)
        late_other = swap(late, "col", step)
        if step > 1:
            size = early.shape[1]
            early = jnp.concatenate((early, early_other, late), axis=1)
            early_items += flipped(early_items, step, size) + flipped(late_items, 0, 2 * size)
            early_cores += [lane + size for lane in early_cores] + [2 * size + rows]
            late, late_items = late_other, flipped(late_items, step)
    total, other_tile, basis = call(
        functools.partial(early_near_kernel, order=early_items),
        (
            jax.ShapeDtypeStruct((width, rows), F32),
            jax.ShapeDtypeStruct(tiles.shape[1:], tiles.dtype),
            jax.ShapeDtypeStruct((rank, rows), basis_out.dtype),
        ),
        (early, own_tile, tiles, basis_out.T),
        [VMEM, VMEM, HBM, HBM],
        scratch=[pltpu.SemaphoreType.DMA((2,))],
        flops=tiles.size * width,
        moved=tiles.size,
    )
    total, core = call(
        functools.partial(
            near_kernel,
            early=flipped(early_items, 1),
            late=late_items,
            cores=(early_cores, early_cores, [rows]),
        ),
        (
            jax.ShapeDtypeStruct((width, rows), F32),
            jax.ShapeDtypeStruct((width, rank), F32),
        ),
        (total, early, early_other, late, own_tile, other_tile),
        [VMEM] * 6,
        flops=tiles.size * width,
        moved=tiles.size,
    )
    out = call(
        functools.partial(last_kernel, late=flipped(late_items, 1), lane=rows),
        jax.ShapeDtypeStruct((width, rows), F32),
        (total, core, late_other, basis, own_tile, other_tile),
        [VMEM] * 6,
        flops=tiles.size * width,
        moved=tiles.size,
    )
    return out.T


def solution(mesh):
    placed = (
        P(("chain", "cell", "col"), None),
        P("cell", None, "col", None),
        P(),
        P(),
        P(),
        P(),
        P("cell", None, None, None),
        P(("cell", "col"), None),
        P(("cell", "col"), None),
    )

    return jax.shard_map(
        body,
        mesh=mesh,
        in_specs=placed,
        out_specs=P(("chain", "cell", "col"), None),
        check_vma=False,
    )
```

```python
import functools

import jax
import jax.numpy as jnp
from jax import lax
from jax.experimental import pallas as pl
from jax.experimental.pallas import tpu as pltpu
from jax.sharding import PartitionSpec as P


REACH = 2
PIECES = 3
CUTS = 2
F32 = jnp.float32
BF16 = jnp.bfloat16
VMEM = pl.BlockSpec(memory_space=pltpu.VMEM)
HBM = pl.BlockSpec(memory_space=pltpu.HBM)
NT = (((1,), (1,)), ((), ()))


def call(kernel, out, inputs, specs, home=VMEM, scratch=(), flops=0, moved=0):
    inputs = [
        pltpu.with_memory_space_constraint(value, pltpu.HBM) if spec is HBM else value
        for value, spec in zip(inputs, specs)
    ]
    return pl.pallas_call(
        kernel,
        out_shape=out,
        in_specs=specs,
        out_specs=jax.tree.map(lambda _: home, out),
        scratch_shapes=list(scratch),
        cost_estimate=pl.CostEstimate(flops=flops, bytes_accessed=moved, transcendentals=0),
        compiler_params=pltpu.CompilerParams(vmem_limit_bytes=16 << 20),
    )(*inputs)


def pieces(value, count):
    out = []
    for _ in range(count):
        out.append(value.astype(BF16))
        value = value - out[-1].astype(F32)
    return out


def twins(value):
    rank = value.shape[1] // 2
    high = value.astype(BF16).astype(F32)
    lane = lax.broadcasted_iota(jnp.int32, value.shape, 1)
    return jnp.where(lane < rank, high, value - high).astype(BF16)


def mixed(tails, mix_ref, group):
    held = jnp.concatenate(tails * PIECES, axis=1)
    return jnp.dot(held, mix_ref[group], preferred_element_type=F32)


def join(ref, at, width):
    high = ref[:, at : at + width].astype(F32)
    return high + ref[:, at + width : at + 2 * width].astype(F32)


def fetch(sources, targets, sems):
    copies = [
        pltpu.make_async_copy(source, target, sems.at[index])
        for index, (source, target) in enumerate(zip(sources, targets))
    ]
    for copy in copies:
        copy.start()
    return copies


def cut(ref):
    lines = ref.shape[0] // CUTS
    return [ref.at[pl.ds(index * lines, lines)] for index in range(CUTS)]


def first_kernel(grad_hbm, basis_hbm, out_ref, own_ref, grad_ref, basis_ref, sems):
    rows = basis_ref.shape[1]
    copies = fetch(
        [*cut(basis_hbm), *cut(grad_hbm)], [*cut(basis_ref), *cut(grad_ref)], sems
    )
    for copy in copies:
        copy.wait()
    rounded = grad_ref[...].astype(BF16)
    out_ref[:, :rows] = rounded
    own_ref[...] = rounded
    basis = basis_ref[...]
    doubled = jnp.concatenate((basis, basis), axis=0)
    partial = lax.dot_general(rounded, doubled, NT, preferred_element_type=F32)
    out_ref[:, rows:] = twins(partial)


def table_kernel(*refs):
    tiles_hbm, inputs, (mix_ref, flag_ref, tiles_ref) = refs[0], refs[1:6], refs[6:9]
    held, sems = refs[9:14], refs[14]
    count_ref, offset_ref, source_ref, far_ref, cores_ref = held
    owner = lax.axis_index("cell")
    slots, rank, _ = cores_ref.shape
    copies = fetch((*inputs, tiles_hbm.at[0]), (*held, tiles_ref), sems)
    for copy in copies[:-1]:
        copy.wait()
    used = far_ref[owner]
    place = lax.axis_index("col")
    steps = [cell_step(place, stage) for stage in range(2)]
    for step in range(4):
        total = jnp.zeros((rank, rank), F32)
        source = owner ^ (steps[0] * (step & 1)) ^ (steps[1] * (step >> 1))
        for slot in range(slots):
            hit = jnp.logical_and(source_ref[owner, slot] == source, slot < used)
            total = total + jnp.where(hit, cores_ref[slot], 0.0)
        total = total.T
        for piece, value in enumerate(pieces(jnp.concatenate((total, total), axis=1), PIECES)):
            for twin in range(2):
                at = (4 * piece + 2 * (step % 2) + twin) * rank
                mix_ref[step // 2, at : at + rank, :] = value
    beyond = owner ^ steps[1]
    asked = beyond + offset_ref[beyond] == owner ^ steps[0]
    beside = offset_ref[owner] + owner == owner ^ steps[0]
    double = count_ref[owner] == 2
    for row, value in enumerate((asked, beside, double)):
        flag_ref[row] = jnp.full(flag_ref.shape[1:], value.astype(F32), F32)
    copies[-1].wait()


def pick(flag_ref, row, yes, no, use=None):
    mask = jnp.broadcast_to(flag_ref[row][:1, :1], yes.shape) > 0.5
    value = jnp.where(mask, yes.astype(F32), no.astype(F32))
    if use is not None:
        value = jnp.where(use > 0.5, value, 0.0)
    return value.astype(BF16)


def second_kernel(flag_ref, mine_ref, near_ref, out_ref, *, rows):
    out_ref[:, :rows] = pick(flag_ref, 0, near_ref[:, :rows], mine_ref[:, :rows])
    tail = mine_ref.shape[1] - rows
    out_ref[:, rows : rows + tail] = mine_ref[:, rows:]
    out_ref[:, rows + tail :] = near_ref[:, rows:]


def early_kernel(mix_ref, mine_ref, near_ref, after_ref, out_ref, *, rows):
    del after_ref
    out_ref[...] = mixed([mine_ref[:, rows:], near_ref[:, rows:]], mix_ref, 0)


def third_kernel(flag_ref, mix_ref, core_ref, near_ref, far_ref, out_ref, *, rows):
    use = jnp.broadcast_to(flag_ref[2][:1, :1], (far_ref.shape[0], rows))
    out_ref[:, :rows] = pick(flag_ref, 1, near_ref[:, :rows], far_ref[:, :rows], use)
    out_ref[:, rows:] = twins(core_ref[...] + mixed([far_ref[:, rows:]], mix_ref, 1))


def stage_kernel(tiles_hbm, tiles_ref, sems):
    for copy in fetch((tiles_hbm.at[0],), (tiles_ref,), sems):
        copy.wait()


def flipped(items, step, at=0):
    return [(lane + at, part, spot ^ step) for lane, part, spot in items]


def near(total, held_ref, tiles, order):
    place = lax.axis_index("col")
    rows = tiles[0].shape[0]
    for lane, part, spot in order:
        columns = pl.ds(pl.multiple_of((place ^ spot) * rows, rows), rows)
        total = total + lax.dot_general(
            held_ref[:, lane : lane + rows],
            tiles[part][:, columns],
            NT,
            preferred_element_type=F32,
        )
    return total


def early_near_kernel(
    held_ref, own_ref, tiles_hbm, basis_hbm, out_ref, tiles_ref, basis_ref, sems, *, order
):
    copies = fetch((tiles_hbm.at[1], basis_hbm), (tiles_ref, basis_ref), sems)
    tiles = (own_ref, tiles_ref)
    ready = [entry for entry in order if entry[1] == 0]
    total = near(jnp.zeros(out_ref.shape, F32), held_ref, tiles, ready)
    for copy in copies:
        copy.wait()
    out_ref[...] = near(total, held_ref, tiles, [entry for entry in order if entry[1] == 1])


def near_kernel(
    sum_ref, mine_ref, early_ref, late_ref, own_ref, tiles_ref, out_ref, core_ref, *, early, late, cores
):
    tiles = (own_ref, tiles_ref)
    out_ref[...] = near(near(sum_ref[...], late_ref, tiles, late), early_ref, tiles, early)
    core = jnp.zeros(core_ref.shape, F32)
    for ref, lanes in zip((mine_ref, early_ref, late_ref), cores):
        for lane in lanes:
            core = core + join(ref, lane, core.shape[1])
    core_ref[...] = core


def last_kernel(
    sum_ref, core_ref, other_ref, basis_ref, own_ref, tiles_ref, out_ref, *, late, lane
):
    core = (core_ref[...] + join(other_ref, lane, core_ref.shape[1])).astype(BF16)
    far = jnp.dot(core, basis_ref[...], preferred_element_type=F32)
    out_ref[...] = near(sum_ref[...] + far, other_ref, (own_ref, tiles_ref), late)


def swap(value, axis, step):
    size = lax.axis_size(axis)
    return lax.ppermute(value, axis, [(i, i ^ step) for i in range(size)])


def cell_step(place, stage):
    return 1 + (place + stage + 1) % 2


def crossed(value, stage):
    cells, parts = lax.axis_size("cell"), lax.axis_size("col")
    pairs = [
        (cell * parts + place, (cell ^ cell_step(place, stage)) * parts + place)
        for cell in range(cells)
        for place in range(parts)
    ]
    return lax.ppermute(value, ("cell", "col"), pairs)


def shifted(value, axis, by):
    size = lax.axis_size(axis)
    return lax.ppermute(value, axis, [(i, i + by) for i in range(size) if 0 <= i + by < size])


def over_small_chain(first, tables, cores, tiles):
    width, length = first.shape
    rows, rank = tiles.shape[1], cores.shape[1]
    beyond = crossed(first, 0)
    mix, flags, own_tile = call(
        table_kernel,
        (
            jax.ShapeDtypeStruct((2, 4 * PIECES * rank, 2 * rank), BF16),
            jax.ShapeDtypeStruct((3, 8, 128), F32),
            jax.ShapeDtypeStruct(tiles.shape[1:], tiles.dtype),
        ),
        (tiles, *tables, cores),
        [HBM] * 6,
        scratch=[
            *(pltpu.SMEM(table.shape, table.dtype) for table in tables),
            pltpu.VMEM(cores.shape, cores.dtype),
            pltpu.SemaphoreType.DMA((6,)),
        ],
        moved=cores.size * 4 + tiles.size,
    )
    second = call(
        functools.partial(second_kernel, rows=rows),
        jax.ShapeDtypeStruct((width, 2 * length - rows), BF16),
        (flags, first, beyond),
        [VMEM] * 3,
        moved=4 * first.size,
    )
    far = crossed(second, 1)
    core = call(
        functools.partial(early_kernel, rows=rows),
        jax.ShapeDtypeStruct((width, 2 * rank), F32),
        (mix, first, beyond, second),
        [VMEM] * 4,
        moved=8 * first.size,
    )
    third = call(
        functools.partial(third_kernel, rows=rows),
        jax.ShapeDtypeStruct((width, length), BF16),
        (flags, mix, core, beyond, far),
        [VMEM] * 5,
        moved=8 * first.size,
    )
    return third, own_tile


def over_long_chain(first, tables, cores, tiles):
    owner = lax.axis_index("cell")
    rows, rank = tiles.shape[1], cores.shape[1]
    own_tile = call(
        stage_kernel,
        jax.ShapeDtypeStruct(tiles.shape[1:], tiles.dtype),
        (tiles,),
        [HBM],
        scratch=[pltpu.SemaphoreType.DMA((1,))],
        moved=tiles.size,
    )
    counts, offsets, sources, used = (table[owner] for table in tables)
    steps = [step for step in range(-REACH, REACH + 1) if step]
    moved = jnp.stack([shifted(first[:, :rows], "cell", -step) for step in steps])
    beside = lax.dynamic_index_in_dim(
        moved, offsets + REACH - (offsets > 0).astype(jnp.int32), 0, keepdims=False
    )
    beside = jnp.where(counts == 2, beside, jnp.zeros_like(beside))
    high, low = first[:, rows : rows + rank], first[:, rows + rank :]
    partial = high.astype(F32) + low.astype(F32)
    table = lax.all_gather(partial[None], "cell", axis=0, tiled=True)
    picked = jnp.take(table, sources, axis=0)
    slots = jnp.arange(cores.shape[0], dtype=jnp.int32)
    masked = jnp.where((slots < used)[:, None, None], cores, jnp.zeros_like(cores))
    core = jnp.einsum("kab,kwb->wa", masked, picked, precision=lax.Precision.HIGHEST)
    return jnp.concatenate((beside, *pieces(core, 2)), axis=1), own_tile


def body(
    grad, near_tiles, tile_count, near_offset, far_src, far_count, far_cores, basis_out, basis_in
):
    rows, width = grad.shape
    rank = basis_in.shape[1]
    cells, parts = lax.axis_size("cell"), lax.axis_size("col")
    first, own = call(
        first_kernel,
        (
            jax.ShapeDtypeStruct((width, rows + 2 * rank), BF16),
            jax.ShapeDtypeStruct((width, rows), BF16),
        ),
        (grad.T, basis_in.T),
        [HBM] * 2,
        scratch=[
            pltpu.VMEM((width, rows), grad.dtype),
            pltpu.VMEM((rank, rows), basis_in.dtype),
            pltpu.SemaphoreType.DMA((2 * CUTS,)),
        ],
        moved=8 * grad.size,
    )
    tables = (tile_count, near_offset, far_src, far_count)
    tiles = near_tiles[0]
    over_cells = over_small_chain if cells == 2 * REACH else over_long_chain
    late, own_tile = over_cells(first, tables, far_cores[0], tiles)
    late_items, early_items = [(0, 1, 0)], [(0, 0, 0)]
    early, early_cores = own, []
    steps = [1 << bit for bit in reversed(range(parts.bit_length() - 1))]
    for step in steps:
        early_other = swap(early, "col", step)
        late_other = swap(late, "col", step)
        if step > 1:
            size = early.shape[1]
            early = jnp.concatenate((early, early_other, late), axis=1)
            early_items += flipped(early_items, step, size) + flipped(late_items, 0, 2 * size)
            early_cores += [lane + size for lane in early_cores] + [2 * size + rows]
            late, late_items = late_other, flipped(late_items, step)
    total, other_tile, basis = call(
        functools.partial(early_near_kernel, order=early_items),
        (
            jax.ShapeDtypeStruct((width, rows), F32),
            jax.ShapeDtypeStruct(tiles.shape[1:], tiles.dtype),
            jax.ShapeDtypeStruct((rank, rows), basis_out.dtype),
        ),
        (early, own_tile, tiles, basis_out.T),
        [VMEM, VMEM, HBM, HBM],
        scratch=[pltpu.SemaphoreType.DMA((2,))],
        flops=tiles.size * width,
        moved=tiles.size,
    )
    total, core = call(
        functools.partial(
            near_kernel,
            early=flipped(early_items, 1),
            late=late_items,
            cores=(early_cores, early_cores, [rows]),
        ),
        (
            jax.ShapeDtypeStruct((width, rows), F32),
            jax.ShapeDtypeStruct((width, rank), F32),
        ),
        (total, early, early_other, late, own_tile, other_tile),
        [VMEM] * 6,
        flops=tiles.size * width,
        moved=tiles.size,
    )
    out = call(
        functools.partial(last_kernel, late=flipped(late_items, 1), lane=rows),
        jax.ShapeDtypeStruct((width, rows), F32),
        (total, core, late_other, basis, own_tile, other_tile),
        [VMEM] * 6,
        flops=tiles.size * width,
        moved=tiles.size,
    )
    return out.T


def solution(mesh):
    placed = (
        P(("chain", "cell", "col"), None),
        P("cell", None, "col", None),
        P(),
        P(),
        P(),
        P(),
        P("cell", None, None, None),
        P(("cell", "col"), None),
        P(("cell", "col"), None),
    )

    return jax.shard_map(
        body,
        mesh=mesh,
        in_specs=placed,
        out_specs=P(("chain", "cell", "col"), None),
        check_vma=False,
    )
```

```python
import functools

import jax
import jax.numpy as jnp
from jax import lax
from jax.experimental import pallas as pl
from jax.experimental.pallas import tpu as pltpu
from jax.sharding import PartitionSpec as P


REACH = 2
PIECES = 3
AHEAD = 2
CUTS = 2
F32 = jnp.float32
BF16 = jnp.bfloat16
VMEM = pl.BlockSpec(memory_space=pltpu.VMEM)
HBM = pl.BlockSpec(memory_space=pltpu.HBM)
NT = (((1,), (1,)), ((), ()))


def call(kernel, out, inputs, specs, home=VMEM, scratch=(), flops=0, moved=0, alias=None):
    inputs = [
        pltpu.with_memory_space_constraint(value, pltpu.HBM) if spec is HBM else value
        for value, spec in zip(inputs, specs)
    ]
    return pl.pallas_call(
        kernel,
        out_shape=out,
        in_specs=specs,
        out_specs=jax.tree.map(lambda _: home, out),
        scratch_shapes=list(scratch),
        input_output_aliases=alias or {},
        cost_estimate=pl.CostEstimate(flops=flops, bytes_accessed=moved, transcendentals=0),
        compiler_params=pltpu.CompilerParams(vmem_limit_bytes=16 << 20),
    )(*inputs)


def pieces(value, count):
    out = []
    for _ in range(count):
        out.append(value.astype(BF16))
        value = value - out[-1].astype(F32)
    return out


def twins(value):
    rank = value.shape[1] // 2
    high = value.astype(BF16).astype(F32)
    lane = lax.broadcasted_iota(jnp.int32, value.shape, 1)
    return jnp.where(lane < rank, high, value - high).astype(BF16)


def mixed(tails, mix_ref, group):
    held = jnp.concatenate(tails * PIECES, axis=1)
    return jnp.dot(held, mix_ref[group], preferred_element_type=F32)


def join(ref, at, width):
    high = ref[:, at : at + width].astype(F32)
    return high + ref[:, at + width : at + 2 * width].astype(F32)


def fetch(sources, targets, sems):
    copies = [
        pltpu.make_async_copy(source, target, sems.at[index])
        for index, (source, target) in enumerate(zip(sources, targets))
    ]
    for copy in copies:
        copy.start()
    return copies


def cut(ref):
    lines = ref.shape[0] // CUTS
    return [ref.at[pl.ds(index * lines, lines)] for index in range(CUTS)]


def first_kernel(grad_hbm, basis_hbm, out_ref, own_ref, grad_ref, basis_ref, sems):
    rows = basis_ref.shape[1]
    copies = fetch(
        [*cut(basis_hbm), *cut(grad_hbm)], [*cut(basis_ref), *cut(grad_ref)], sems
    )
    for copy in copies:
        copy.wait()
    rounded = grad_ref[...].astype(BF16)
    out_ref[:, :rows] = rounded
    own_ref[...] = rounded
    basis = basis_ref[...]
    doubled = jnp.concatenate((basis, basis), axis=0)
    partial = lax.dot_general(rounded, doubled, NT, preferred_element_type=F32)
    out_ref[:, rows:] = twins(partial)


def table_kernel(*refs):
    tiles_hbm, inputs, (mix_ref, flag_ref, tiles_ref) = refs[0], refs[1:6], refs[6:9]
    held, sems = refs[9:14], refs[14]
    count_ref, offset_ref, source_ref, far_ref, cores_ref = held
    owner = lax.axis_index("cell")
    slots, rank, _ = cores_ref.shape
    copies = fetch((*inputs, tiles_hbm.at[0]), (*held, tiles_ref), sems)
    for copy in copies[:-1]:
        copy.wait()
    used = far_ref[owner]
    place = lax.axis_index("col")
    steps = [cell_step(place, stage) for stage in range(2)]
    for step in range(4):
        total = jnp.zeros((rank, rank), F32)
        source = owner ^ (steps[0] * (step & 1)) ^ (steps[1] * (step >> 1))
        for slot in range(slots):
            hit = jnp.logical_and(source_ref[owner, slot] == source, slot < used)
            total = total + jnp.where(hit, cores_ref[slot], 0.0)
        total = total.T
        for piece, value in enumerate(pieces(jnp.concatenate((total, total), axis=1), PIECES)):
            for twin in range(2):
                at = (4 * piece + 2 * (step % 2) + twin) * rank
                mix_ref[step // 2, at : at + rank, :] = value
    beyond = owner ^ steps[1]
    asked = beyond + offset_ref[beyond] == owner ^ steps[0]
    beside = offset_ref[owner] + owner == owner ^ steps[0]
    double = count_ref[owner] == 2
    for row, value in enumerate((asked, beside, double)):
        flag_ref[row] = jnp.full(flag_ref.shape[1:], value.astype(F32), F32)
    copies[-1].wait()


def pick(flag_ref, row, yes, no, use=None):
    mask = jnp.broadcast_to(flag_ref[row][:1, :1], yes.shape) > 0.5
    value = jnp.where(mask, yes.astype(F32), no.astype(F32))
    if use is not None:
        value = jnp.where(use > 0.5, value, 0.0)
    return value.astype(BF16)


def second_kernel(flag_ref, mine_ref, near_ref, out_ref, *, rows):
    out_ref[:, :rows] = pick(flag_ref, 0, near_ref[:, :rows], mine_ref[:, :rows])
    tail = mine_ref.shape[1] - rows
    out_ref[:, rows : rows + tail] = mine_ref[:, rows:]
    out_ref[:, rows + tail :] = near_ref[:, rows:]


def leads():
    return lax.axis_index("col") % 2 == 1


def early_kernel(
    mix_ref, mine_ref, near_ref, after_ref, tiles_hbm, out_ref, tiles_ref, sems, *, rows
):
    del after_ref

    @pl.when(leads())
    def _():
        pltpu.make_async_copy(tiles_hbm.at[1], tiles_ref, sems.at[0]).start()

    out_ref[...] = mixed([mine_ref[:, rows:], near_ref[:, rows:]], mix_ref, 0)

    @pl.when(leads())
    def _():
        pltpu.make_async_copy(tiles_hbm.at[1], tiles_ref, sems.at[0]).wait()


def third_kernel(flag_ref, mix_ref, core_ref, near_ref, far_ref, out_ref, *, rows):
    use = jnp.broadcast_to(flag_ref[2][:1, :1], (far_ref.shape[0], rows))
    out_ref[:, :rows] = pick(flag_ref, 1, near_ref[:, :rows], far_ref[:, :rows], use)
    out_ref[:, rows:] = twins(core_ref[...] + mixed([far_ref[:, rows:]], mix_ref, 1))


def stage_kernel(tiles_hbm, own_ref, other_ref, sems):
    for copy in fetch((tiles_hbm.at[0], tiles_hbm.at[1]), (own_ref, other_ref), sems):
        copy.wait()


def flipped(items, step, at=0):
    return [(lane + at, part, spot ^ step) for lane, part, spot in items]


def near(total, held_ref, tiles, order):
    place = lax.axis_index("col")
    rows = tiles[0].shape[0]
    for lane, part, spot in order:
        columns = pl.ds(pl.multiple_of((place ^ spot) * rows, rows), rows)
        total = total + lax.dot_general(
            held_ref[:, lane : lane + rows],
            tiles[part][:, columns],
            NT,
            preferred_element_type=F32,
        )
    return total


def early_near_kernel(
    held_ref, own_ref, held_tiles_ref, tiles_hbm, basis_hbm, out_ref, tiles_ref, basis_ref, sems, *, order
):
    del held_tiles_ref
    follows = jnp.logical_not(leads())

    @pl.when(follows)
    def _():
        pltpu.make_async_copy(tiles_hbm.at[1], tiles_ref, sems.at[0]).start()

    basis_copy = pltpu.make_async_copy(basis_hbm, basis_ref, sems.at[1])
    basis_copy.start()
    tiles = (own_ref, tiles_ref)
    ready = [entry for entry in order if entry[1] == 0]
    total = near(jnp.zeros(out_ref.shape, F32), held_ref, tiles, ready)

    @pl.when(follows)
    def _():
        pltpu.make_async_copy(tiles_hbm.at[1], tiles_ref, sems.at[0]).wait()

    out_ref[...] = near(total, held_ref, tiles, [entry for entry in order if entry[1] == 1])
    basis_copy.wait()


def middle_kernel(sum_ref, early_ref, own_ref, tiles_ref, out_ref, *, order):
    out_ref[...] = sum_ref[...]

    @pl.when(leads())
    def _():
        out_ref[...] = near(sum_ref[...], early_ref, (own_ref, tiles_ref), order)


def near_kernel(
    sum_ref, mine_ref, early_ref, late_ref, own_ref, tiles_ref, out_ref, core_ref, *, early, late, cores
):
    tiles = (own_ref, tiles_ref)
    total = near(sum_ref[...], late_ref, tiles, late)
    out_ref[...] = near(total, early_ref, tiles, early[AHEAD:])

    @pl.when(jnp.logical_not(leads()))
    def _():
        out_ref[...] = near(out_ref[...], early_ref, tiles, early[:AHEAD])

    core = jnp.zeros(core_ref.shape, F32)
    for ref, lanes in zip((mine_ref, early_ref, late_ref), cores):
        for lane in lanes:
            core = core + join(ref, lane, core.shape[1])
    core_ref[...] = core


def last_kernel(
    sum_ref, core_ref, other_ref, basis_ref, own_ref, tiles_ref, out_ref, *, late, lane
):
    total = near(sum_ref[...], other_ref, (own_ref, tiles_ref), late)
    core = (core_ref[...] + join(other_ref, lane, core_ref.shape[1])).astype(BF16)
    out_ref[...] = total + jnp.dot(core, basis_ref[...], preferred_element_type=F32)


def swap(value, axis, step):
    size = lax.axis_size(axis)
    return lax.ppermute(value, axis, [(i, i ^ step) for i in range(size)])


def cell_step(place, stage):
    return 1 + (place + stage + 1) % 2


def crossed(value, stage):
    cells, parts = lax.axis_size("cell"), lax.axis_size("col")
    pairs = [
        (cell * parts + place, (cell ^ cell_step(place, stage)) * parts + place)
        for cell in range(cells)
        for place in range(parts)
    ]
    return lax.ppermute(value, ("cell", "col"), pairs)


def shifted(value, axis, by):
    size = lax.axis_size(axis)
    return lax.ppermute(value, axis, [(i, i + by) for i in range(size) if 0 <= i + by < size])


def over_small_chain(first, tables, cores, tiles):
    width, length = first.shape
    rows, rank = tiles.shape[1], cores.shape[1]
    beyond = crossed(first, 0)
    mix, flags, own_tile = call(
        table_kernel,
        (
            jax.ShapeDtypeStruct((2, 4 * PIECES * rank, 2 * rank), BF16),
            jax.ShapeDtypeStruct((3, 8, 128), F32),
            jax.ShapeDtypeStruct(tiles.shape[1:], tiles.dtype),
        ),
        (tiles, *tables, cores),
        [HBM] * 6,
        scratch=[
            *(pltpu.SMEM(table.shape, table.dtype) for table in tables),
            pltpu.VMEM(cores.shape, cores.dtype),
            pltpu.SemaphoreType.DMA((6,)),
        ],
        moved=cores.size * 4 + tiles.size,
    )
    second = call(
        functools.partial(second_kernel, rows=rows),
        jax.ShapeDtypeStruct((width, 2 * length - rows), BF16),
        (flags, first, beyond),
        [VMEM] * 3,
        moved=4 * first.size,
    )
    far = crossed(second, 1)
    core, other_tile = call(
        functools.partial(early_kernel, rows=rows),
        (
            jax.ShapeDtypeStruct((width, 2 * rank), F32),
            jax.ShapeDtypeStruct(tiles.shape[1:], tiles.dtype),
        ),
        (mix, first, beyond, second, tiles),
        [VMEM] * 4 + [HBM],
        scratch=[pltpu.SemaphoreType.DMA((1,))],
        moved=8 * first.size,
    )
    third = call(
        functools.partial(third_kernel, rows=rows),
        jax.ShapeDtypeStruct((width, length), BF16),
        (flags, mix, core, beyond, far),
        [VMEM] * 5,
        moved=8 * first.size,
    )
    return third, own_tile, other_tile


def over_long_chain(first, tables, cores, tiles):
    owner = lax.axis_index("cell")
    rows, rank = tiles.shape[1], cores.shape[1]
    own_tile, other_tile = call(
        stage_kernel,
        (jax.ShapeDtypeStruct(tiles.shape[1:], tiles.dtype),) * 2,
        (tiles,),
        [HBM],
        scratch=[pltpu.SemaphoreType.DMA((2,))],
        moved=tiles.size,
    )
    counts, offsets, sources, used = (table[owner] for table in tables)
    steps = [step for step in range(-REACH, REACH + 1) if step]
    moved = jnp.stack([shifted(first[:, :rows], "cell", -step) for step in steps])
    beside = lax.dynamic_index_in_dim(
        moved, offsets + REACH - (offsets > 0).astype(jnp.int32), 0, keepdims=False
    )
    beside = jnp.where(counts == 2, beside, jnp.zeros_like(beside))
    high, low = first[:, rows : rows + rank], first[:, rows + rank :]
    partial = high.astype(F32) + low.astype(F32)
    table = lax.all_gather(partial[None], "cell", axis=0, tiled=True)
    picked = jnp.take(table, sources, axis=0)
    slots = jnp.arange(cores.shape[0], dtype=jnp.int32)
    masked = jnp.where((slots < used)[:, None, None], cores, jnp.zeros_like(cores))
    core = jnp.einsum("kab,kwb->wa", masked, picked, precision=lax.Precision.HIGHEST)
    return jnp.concatenate((beside, *pieces(core, 2)), axis=1), own_tile, other_tile


def body(
    grad, near_tiles, tile_count, near_offset, far_src, far_count, far_cores, basis_out, basis_in
):
    rows, width = grad.shape
    rank = basis_in.shape[1]
    cells, parts = lax.axis_size("cell"), lax.axis_size("col")
    first, own = call(
        first_kernel,
        (
            jax.ShapeDtypeStruct((width, rows + 2 * rank), BF16),
            jax.ShapeDtypeStruct((width, rows), BF16),
        ),
        (grad.T, basis_in.T),
        [HBM] * 2,
        scratch=[
            pltpu.VMEM((width, rows), grad.dtype),
            pltpu.VMEM((rank, rows), basis_in.dtype),
            pltpu.SemaphoreType.DMA((2 * CUTS,)),
        ],
        moved=8 * grad.size,
    )
    tables = (tile_count, near_offset, far_src, far_count)
    tiles = near_tiles[0]
    over_cells = over_small_chain if cells == 2 * REACH else over_long_chain
    late, own_tile, other_tile = over_cells(first, tables, far_cores[0], tiles)
    late_items, early_items = [(0, 1, 0)], [(0, 0, 0)]
    early, early_cores = own, []
    steps = [1 << bit for bit in reversed(range(parts.bit_length() - 1))]
    for step in steps:
        early_other = swap(early, "col", step)
        late_other = swap(late, "col", step)
        if step > 1:
            size = early.shape[1]
            early = jnp.concatenate((early, early_other, late), axis=1)
            early_items += flipped(early_items, step, size) + flipped(late_items, 0, 2 * size)
            early_cores += [lane + size for lane in early_cores] + [2 * size + rows]
            late, late_items = late_other, flipped(late_items, step)
    total, other_tile, basis = call(
        functools.partial(early_near_kernel, order=early_items),
        (
            jax.ShapeDtypeStruct((width, rows), F32),
            jax.ShapeDtypeStruct(tiles.shape[1:], tiles.dtype),
            jax.ShapeDtypeStruct((rank, rows), basis_out.dtype),
        ),
        (early, own_tile, other_tile, tiles, basis_out.T),
        [VMEM, VMEM, VMEM, HBM, HBM],
        alias={2: 1},
        scratch=[pltpu.SemaphoreType.DMA((2,))],
        flops=tiles.size * width,
        moved=tiles.size,
    )
    across = flipped(early_items, 1)
    total = call(
        functools.partial(middle_kernel, order=across[:AHEAD]),
        jax.ShapeDtypeStruct((width, rows), F32),
        (total, early_other, own_tile, other_tile),
        [VMEM] * 4,
        flops=tiles.size * width,
        moved=tiles.size,
    )
    total, core = call(
        functools.partial(
            near_kernel,
            early=across,
            late=late_items,
            cores=(early_cores, early_cores, [rows]),
        ),
        (
            jax.ShapeDtypeStruct((width, rows), F32),
            jax.ShapeDtypeStruct((width, rank), F32),
        ),
        (total, early, early_other, late, own_tile, other_tile),
        [VMEM] * 6,
        flops=tiles.size * width,
        moved=tiles.size,
    )
    out = call(
        functools.partial(last_kernel, late=flipped(late_items, 1), lane=rows),
        jax.ShapeDtypeStruct((width, rows), F32),
        (total, core, late_other, basis, own_tile, other_tile),
        [VMEM] * 6,
        flops=tiles.size * width,
        moved=tiles.size,
    )
    return out.T


def solution(mesh):
    placed = (
        P(("chain", "cell", "col"), None),
        P("cell", None, "col", None),
        P(),
        P(),
        P(),
        P(),
        P("cell", None, None, None),
        P(("cell", "col"), None),
        P(("cell", "col"), None),
    )

    return jax.shard_map(
        body,
        mesh=mesh,
        in_specs=placed,
        out_specs=P(("chain", "cell", "col"), None),
        check_vma=False,
    )
```

```python
import functools

import jax
import jax.numpy as jnp
from jax import lax
from jax.experimental import pallas as pl
from jax.experimental.pallas import tpu as pltpu
from jax.sharding import PartitionSpec as P


REACH = 2
PIECES = 3
CUTS = 4
F32 = jnp.float32
BF16 = jnp.bfloat16
VMEM = pl.BlockSpec(memory_space=pltpu.VMEM)
HBM = pl.BlockSpec(memory_space=pltpu.HBM)
NT = (((1,), (1,)), ((), ()))


def call(kernel, out, inputs, specs, home=VMEM, scratch=(), flops=0, moved=0):
    inputs = [
        pltpu.with_memory_space_constraint(value, pltpu.HBM) if spec is HBM else value
        for value, spec in zip(inputs, specs)
    ]
    return pl.pallas_call(
        kernel,
        out_shape=out,
        in_specs=specs,
        out_specs=jax.tree.map(lambda _: home, out),
        scratch_shapes=list(scratch),
        cost_estimate=pl.CostEstimate(flops=flops, bytes_accessed=moved, transcendentals=0),
        compiler_params=pltpu.CompilerParams(vmem_limit_bytes=16 << 20),
    )(*inputs)


def pieces(value, count):
    out = []
    for _ in range(count):
        out.append(value.astype(BF16))
        value = value - out[-1].astype(F32)
    return out


def twins(value):
    rank = value.shape[1] // 2
    high = value.astype(BF16).astype(F32)
    lane = lax.broadcasted_iota(jnp.int32, value.shape, 1)
    return jnp.where(lane < rank, high, value - high).astype(BF16)


def mixed(tails, mix_ref, group):
    held = jnp.concatenate(tails * PIECES, axis=1)
    return jnp.dot(held, mix_ref[group], preferred_element_type=F32)


def join(ref, at, width):
    high = ref[:, at : at + width].astype(F32)
    return high + ref[:, at + width : at + 2 * width].astype(F32)


def fetch(sources, targets, sems):
    copies = [
        pltpu.make_async_copy(source, target, sems.at[index])
        for index, (source, target) in enumerate(zip(sources, targets))
    ]
    for copy in copies:
        copy.start()
    return copies


def cut(ref):
    lines = ref.shape[0] // CUTS
    return [ref.at[pl.ds(index * lines, lines)] for index in range(CUTS)]


def first_kernel(grad_hbm, basis_hbm, out_ref, own_ref, grad_ref, basis_ref, sems):
    rows = basis_ref.shape[1]
    copies = fetch(
        [*cut(basis_hbm), *cut(grad_hbm)], [*cut(basis_ref), *cut(grad_ref)], sems
    )
    for copy in copies:
        copy.wait()
    rounded = grad_ref[...].astype(BF16)
    basis = basis_ref[...]
    doubled = jnp.concatenate((basis, basis), axis=0)
    partial = lax.dot_general(rounded, doubled, NT, preferred_element_type=F32)
    out_ref[:, rows:] = twins(partial)
    out_ref[:, :rows] = rounded
    own_ref[...] = rounded


def table_kernel(*refs):
    tiles_hbm, inputs, (mix_ref, flag_ref, tiles_ref) = refs[0], refs[1:6], refs[6:9]
    held, sems = refs[9:14], refs[14]
    count_ref, offset_ref, source_ref, far_ref, cores_ref = held
    owner = lax.axis_index("cell")
    slots, rank, _ = cores_ref.shape
    copies = fetch((*inputs, tiles_hbm.at[0]), (*held, tiles_ref), sems)
    for copy in copies[:-1]:
        copy.wait()
    used = far_ref[owner]
    place = lax.axis_index("col")
    steps = [cell_step(place, stage) for stage in range(2)]
    for step in range(4):
        total = jnp.zeros((rank, rank), F32)
        source = owner ^ (steps[0] * (step & 1)) ^ (steps[1] * (step >> 1))
        for slot in range(slots):
            hit = jnp.logical_and(source_ref[owner, slot] == source, slot < used)
            total = total + jnp.where(hit, cores_ref[slot], 0.0)
        total = total.T
        for piece, value in enumerate(pieces(jnp.concatenate((total, total), axis=1), PIECES)):
            for twin in range(2):
                at = (4 * piece + 2 * (step % 2) + twin) * rank
                mix_ref[step // 2, at : at + rank, :] = value
    beyond = owner ^ steps[1]
    asked = beyond + offset_ref[beyond] == owner ^ steps[0]
    beside = offset_ref[owner] + owner == owner ^ steps[0]
    double = count_ref[owner] == 2
    for row, value in enumerate((asked, beside, double)):
        flag_ref[row] = jnp.full(flag_ref.shape[1:], value.astype(F32), F32)
    copies[-1].wait()


def pick(flag_ref, row, yes, no, use=None):
    mask = jnp.broadcast_to(flag_ref[row][:1, :1], yes.shape) > 0.5
    value = jnp.where(mask, yes.astype(F32), no.astype(F32))
    if use is not None:
        value = jnp.where(use > 0.5, value, 0.0)
    return value.astype(BF16)


def second_kernel(flag_ref, mine_ref, near_ref, out_ref, *, rows):
    out_ref[:, :rows] = pick(flag_ref, 0, near_ref[:, :rows], mine_ref[:, :rows])
    tail = mine_ref.shape[1] - rows
    out_ref[:, rows : rows + tail] = mine_ref[:, rows:]
    out_ref[:, rows + tail :] = near_ref[:, rows:]


def early_kernel(mix_ref, mine_ref, near_ref, after_ref, out_ref, *, rows):
    del after_ref
    out_ref[...] = mixed([mine_ref[:, rows:], near_ref[:, rows:]], mix_ref, 0)


def third_kernel(flag_ref, mix_ref, core_ref, near_ref, far_ref, out_ref, *, rows):
    use = jnp.broadcast_to(flag_ref[2][:1, :1], (far_ref.shape[0], rows))
    out_ref[:, :rows] = pick(flag_ref, 1, near_ref[:, :rows], far_ref[:, :rows], use)
    out_ref[:, rows:] = twins(core_ref[...] + mixed([far_ref[:, rows:]], mix_ref, 1))


def stage_kernel(tiles_hbm, tiles_ref, sems):
    for copy in fetch((tiles_hbm.at[0],), (tiles_ref,), sems):
        copy.wait()


def flipped(items, step, at=0):
    return [(lane + at, part, spot ^ step) for lane, part, spot in items]


def near(total, held_ref, tiles, order):
    place = lax.axis_index("col")
    rows = tiles[0].shape[0]
    for lane, part, spot in order:
        columns = pl.ds(pl.multiple_of((place ^ spot) * rows, rows), rows)
        total = total + lax.dot_general(
            held_ref[:, lane : lane + rows],
            tiles[part][:, columns],
            NT,
            preferred_element_type=F32,
        )
    return total


def early_near_kernel(
    held_ref, own_ref, tiles_hbm, basis_hbm, out_ref, tiles_ref, basis_ref, sems, *, order
):
    copies = fetch((tiles_hbm.at[1], basis_hbm), (tiles_ref, basis_ref), sems)
    tiles = (own_ref, tiles_ref)
    ready = [entry for entry in order if entry[1] == 0]
    total = near(jnp.zeros(out_ref.shape, F32), held_ref, tiles, ready)
    for copy in copies:
        copy.wait()
    out_ref[...] = near(total, held_ref, tiles, [entry for entry in order if entry[1] == 1])


def near_kernel(
    sum_ref, mine_ref, early_ref, late_ref, own_ref, tiles_ref, out_ref, core_ref, *, early, late, cores
):
    tiles = (own_ref, tiles_ref)
    out_ref[...] = near(near(sum_ref[...], early_ref, tiles, early), late_ref, tiles, late)
    core = jnp.zeros(core_ref.shape, F32)
    for ref, lanes in zip((mine_ref, early_ref, late_ref), cores):
        for lane in lanes:
            core = core + join(ref, lane, core.shape[1])
    core_ref[...] = core


def last_kernel(
    sum_ref, core_ref, other_ref, basis_ref, own_ref, tiles_ref, out_ref, *, late, lane
):
    total = near(sum_ref[...], other_ref, (own_ref, tiles_ref), late)
    core = (core_ref[...] + join(other_ref, lane, core_ref.shape[1])).astype(BF16)
    out_ref[...] = total + jnp.dot(core, basis_ref[...], preferred_element_type=F32)


def swap(value, axis, step):
    size = lax.axis_size(axis)
    return lax.ppermute(value, axis, [(i, i ^ step) for i in range(size)])


def cell_step(place, stage):
    return 1 + (place + stage + 1) % 2


def crossed(value, stage):
    cells, parts = lax.axis_size("cell"), lax.axis_size("col")
    pairs = [
        (cell * parts + place, (cell ^ cell_step(place, stage)) * parts + place)
        for cell in range(cells)
        for place in range(parts)
    ]
    return lax.ppermute(value, ("cell", "col"), pairs)


def shifted(value, axis, by):
    size = lax.axis_size(axis)
    return lax.ppermute(value, axis, [(i, i + by) for i in range(size) if 0 <= i + by < size])


def over_small_chain(first, tables, cores, tiles):
    width, length = first.shape
    rows, rank = tiles.shape[1], cores.shape[1]
    beyond = crossed(first, 0)
    mix, flags, own_tile = call(
        table_kernel,
        (
            jax.ShapeDtypeStruct((2, 4 * PIECES * rank, 2 * rank), BF16),
            jax.ShapeDtypeStruct((3, 8, 128), F32),
            jax.ShapeDtypeStruct(tiles.shape[1:], tiles.dtype),
        ),
        (tiles, *tables, cores),
        [HBM] * 6,
        scratch=[
            *(pltpu.SMEM(table.shape, table.dtype) for table in tables),
            pltpu.VMEM(cores.shape, cores.dtype),
            pltpu.SemaphoreType.DMA((6,)),
        ],
        moved=cores.size * 4 + tiles.size,
    )
    second = call(
        functools.partial(second_kernel, rows=rows),
        jax.ShapeDtypeStruct((width, 2 * length - rows), BF16),
        (flags, first, beyond),
        [VMEM] * 3,
        moved=4 * first.size,
    )
    far = crossed(second, 1)
    core = call(
        functools.partial(early_kernel, rows=rows),
        jax.ShapeDtypeStruct((width, 2 * rank), F32),
        (mix, first, beyond, second),
        [VMEM] * 4,
        moved=8 * first.size,
    )
    third = call(
        functools.partial(third_kernel, rows=rows),
        jax.ShapeDtypeStruct((width, length), BF16),
        (flags, mix, core, beyond, far),
        [VMEM] * 5,
        moved=8 * first.size,
    )
    return third, own_tile


def over_long_chain(first, tables, cores, tiles):
    owner = lax.axis_index("cell")
    rows, rank = tiles.shape[1], cores.shape[1]
    own_tile = call(
        stage_kernel,
        jax.ShapeDtypeStruct(tiles.shape[1:], tiles.dtype),
        (tiles,),
        [HBM],
        scratch=[pltpu.SemaphoreType.DMA((1,))],
        moved=tiles.size,
    )
    counts, offsets, sources, used = (table[owner] for table in tables)
    steps = [step for step in range(-REACH, REACH + 1) if step]
    moved = jnp.stack([shifted(first[:, :rows], "cell", -step) for step in steps])
    beside = lax.dynamic_index_in_dim(
        moved, offsets + REACH - (offsets > 0).astype(jnp.int32), 0, keepdims=False
    )
    beside = jnp.where(counts == 2, beside, jnp.zeros_like(beside))
    high, low = first[:, rows : rows + rank], first[:, rows + rank :]
    partial = high.astype(F32) + low.astype(F32)
    table = lax.all_gather(partial[None], "cell", axis=0, tiled=True)
    picked = jnp.take(table, sources, axis=0)
    slots = jnp.arange(cores.shape[0], dtype=jnp.int32)
    masked = jnp.where((slots < used)[:, None, None], cores, jnp.zeros_like(cores))
    core = jnp.einsum("kab,kwb->wa", masked, picked, precision=lax.Precision.HIGHEST)
    return jnp.concatenate((beside, *pieces(core, 2)), axis=1), own_tile


def body(
    grad, near_tiles, tile_count, near_offset, far_src, far_count, far_cores, basis_out, basis_in
):
    rows, width = grad.shape
    rank = basis_in.shape[1]
    cells, parts = lax.axis_size("cell"), lax.axis_size("col")
    first, own = call(
        first_kernel,
        (
            jax.ShapeDtypeStruct((width, rows + 2 * rank), BF16),
            jax.ShapeDtypeStruct((width, rows), BF16),
        ),
        (grad.T, basis_in.T),
        [HBM] * 2,
        scratch=[
            pltpu.VMEM((width, rows), grad.dtype),
            pltpu.VMEM((rank, rows), basis_in.dtype),
            pltpu.SemaphoreType.DMA((2 * CUTS,)),
        ],
        moved=8 * grad.size,
    )
    tables = (tile_count, near_offset, far_src, far_count)
    tiles = near_tiles[0]
    over_cells = over_small_chain if cells == 2 * REACH else over_long_chain
    late, own_tile = over_cells(first, tables, far_cores[0], tiles)
    late_items, early_items = [(0, 1, 0)], [(0, 0, 0)]
    early, early_cores = own, []
    steps = [1 << bit for bit in reversed(range(parts.bit_length() - 1))]
    for step in steps:
        early_other = swap(early, "col", step)
        late_other = swap(late, "col", step)
        if step > 1:
            size = early.shape[1]
            early = jnp.concatenate((early, early_other, late), axis=1)
            early_items += flipped(early_items, step, size) + flipped(late_items, 0, 2 * size)
            early_cores += [lane + size for lane in early_cores] + [2 * size + rows]
            late, late_items = late_other, flipped(late_items, step)
    total, other_tile, basis = call(
        functools.partial(early_near_kernel, order=early_items),
        (
            jax.ShapeDtypeStruct((width, rows), F32),
            jax.ShapeDtypeStruct(tiles.shape[1:], tiles.dtype),
            jax.ShapeDtypeStruct((rank, rows), basis_out.dtype),
        ),
        (early, own_tile, tiles, basis_out.T),
        [VMEM, VMEM, HBM, HBM],
        scratch=[pltpu.SemaphoreType.DMA((2,))],
        flops=tiles.size * width,
        moved=tiles.size,
    )
    total, core = call(
        functools.partial(
            near_kernel,
            early=flipped(early_items, 1),
            late=late_items,
            cores=(early_cores, early_cores, [rows]),
        ),
        (
            jax.ShapeDtypeStruct((width, rows), F32),
            jax.ShapeDtypeStruct((width, rank), F32),
        ),
        (total, early, early_other, late, own_tile, other_tile),
        [VMEM] * 6,
        flops=tiles.size * width,
        moved=tiles.size,
    )
    out = call(
        functools.partial(last_kernel, late=flipped(late_items, 1), lane=rows),
        jax.ShapeDtypeStruct((width, rows), F32),
        (total, core, late_other, basis, own_tile, other_tile),
        [VMEM] * 6,
        flops=tiles.size * width,
        moved=tiles.size,
    )
    return out.T


def solution(mesh):
    placed = (
        P(("chain", "cell", "col"), None),
        P("cell", None, "col", None),
        P(),
        P(),
        P(),
        P(),
        P("cell", None, None, None),
        P(("cell", "col"), None),
        P(("cell", "col"), None),
    )

    return jax.shard_map(
        body,
        mesh=mesh,
        in_specs=placed,
        out_specs=P(("chain", "cell", "col"), None),
        check_vma=False,
    )
```
